32 devices in a mesh: groups: 2 (over x), expert: 8 (over z, y), dp: 2 (over core).
Axes of the slice: x: 2, y: 2, z: 4, core: 2. Of those that a mesh axis runs over, the one named last changes fastest.
Arguments:
- tokens: bfloat16 [1024, 2048], P(('groups', 'expert', 'dp')), parts along dimension 0, may hold values from -6 to 6
- route_ids: int32 [1024, 8], P(('groups', 'expert', 'dp')), parts along dimension 0, may hold values from 0 to 15, as said below
- route_slots: int32 [1024, 8], P(('groups', 'expert', 'dp')), parts along dimension 0, may hold values from 0 to 19, as said below
- route_gates: float32 [1024, 8], P(('groups', 'expert', 'dp')), parts along dimension 0, may hold values from 0.05 to 0.35
- out_cotangent: bfloat16 [1024, 2048], P(('groups', 'expert', 'dp')), parts along dimension 0, may hold values from -6 to 6
- gate_up_weight: bfloat16 [16, 2, 2048, 768], P('expert', None, None, 'dp'), may hold values from -0.125 to 0.125
- w_down: bfloat16 [16, 768, 2048], P('expert', 'dp'), may hold values from -0.21875 to 0.21875
- input_factor: float32 [16, 2, 8, 2048], P('expert'), may hold values from -0.125 to 0.125
- output_factor: float32 [16, 2, 8, 768], P('expert', None, None, 'dp'), may hold values from -0.5 to 0.5
- gains: float32 [16, 2, 768], P('expert', None, 'dp'), may hold values from 0.5 to 1.5
- in_moment: float32 [16, 2, 8, 2048], P('expert', None, None, 'dp'), may hold values from -400 to 400
- out_moment: float32 [16, 2, 8, 768], P('expert', None, None, 'dp'), may hold values from -400 to 400
- gain_moment: float32 [16, 2, 768], P('expert', None, 'dp'), may hold values from -0.3 to 0.3
Outputs:
- mixed: bfloat16 [1024, 2048], P(('groups', 'expert', 'dp')), parts along dimension 0
- token_grad: bfloat16 [1024, 2048], P(('groups', 'expert', 'dp')), parts along dimension 0
- new_in: float32 [32, 2, 8, 2048], P(('groups', 'expert')), parts along dimension 0
- new_in_moment: float32 [32, 2, 8, 2048], P(('groups', 'expert'), None, None, 'dp'), parts along dimension 0
- new_out: float32 [32, 2, 8, 768], P(('groups', 'expert'), None, None, 'dp'), parts along dimension 0
- new_out_moment: float32 [32, 2, 8, 768], P(('groups', 'expert'), None, None, 'dp'), parts along dimension 0
- new_gains: float32 [32, 2, 768], P(('groups', 'expert'), None, 'dp'), parts along dimension 0
- new_gain_moment: float32 [32, 2, 768], P(('groups', 'expert'), None, 'dp'), parts along dimension 0
The draws below stay inside these ranges and needn't reach their ends.
There are 2 independent parts, one for each index of `groups`. The reference program is written for one: setup_inputs(seed, part) draws one part's arguments, and reference() takes and returns one part's arrays. A program takes and returns all parts, laid end to end along the dimension named above; an argument that names none is the same for every part. Nothing has to cross between parts.
Inputs may be any that keep to these rules, and one draw needn't show every extreme that they name: `route_ids`: the 8 experts of one token are different. Within one block of 32 tokens no expert is named more than 20 times, and one expert is named exactly 20 times in every block. `route_slots`: within one block of 32 tokens the slots of the n choices that name one expert are 0 to n - 1, each once.
All inputs are finite; a program needn't handle non-finite values.
Results may differ from the reference program's by a relative error of at most 0.012.
Values may be sent and summed in bfloat16 or wider, within the bound.
A program may use at most 128 MiB of HBM per device.

```python
import math
import jax
import jax.numpy as jnp
from jax import lax

D = 2048
FF = 768
TOP = 8
RANK = 8
TOK_DEV = 32
EXPERTS = 16
CAP = 20
TOKENS = 512
N_DP = 2


def route_block(base_key, hot_expert, block_id):
    block_key = jax.random.fold_in(base_key, 1000 + block_id)
    key_second, key_order, key_tokens, key_within = jax.random.split(block_key, 4)
    unit_count = EXPERTS * CAP
    assigned = TOK_DEV * TOP
    second_expert = jax.random.randint(key_second, (), 0, EXPERTS)
    unit_owner = jnp.arange(unit_count, dtype=jnp.int32) // CAP
    forced = (unit_owner == hot_expert) | (unit_owner == second_expert)
    shuffled = jax.random.permutation(key_order, unit_count).astype(jnp.int32)
    priority = jnp.where(forced, jnp.arange(unit_count, dtype=jnp.int32) - unit_count, shuffled)
    unit_rank = jnp.argsort(jnp.argsort(priority)).astype(jnp.int32)
    kept = (unit_rank < assigned).astype(jnp.int32)
    expert_load = jnp.sum(kept.reshape(EXPERTS, CAP), axis=1).astype(jnp.int32)
    load_ends = jnp.cumsum(expert_load).astype(jnp.int32)
    entry_index = jnp.arange(assigned, dtype=jnp.int32)
    entry_expert = jnp.sum((load_ends[None, :] <= entry_index[:, None]).astype(jnp.int32), axis=1).astype(jnp.int32)
    load_starts = load_ends - expert_load
    entry_slot = entry_index - load_starts[entry_expert]
    table_expert = entry_expert.reshape(TOP, TOK_DEV).T
    table_slot = entry_slot.reshape(TOP, TOK_DEV).T
    token_order = jax.random.permutation(key_tokens, TOK_DEV)
    table_expert = table_expert[token_order]
    table_slot = table_slot[token_order]
    within = jax.random.randint(key_within, (TOK_DEV, TOP), 0, 1 << 20) * TOP + jnp.arange(TOP, dtype=jnp.int32)[None, :]
    column_order = jnp.argsort(within, axis=1)
    table_expert = jnp.take_along_axis(table_expert, column_order, axis=1)
    table_slot = jnp.take_along_axis(table_slot, column_order, axis=1)
    return (table_expert.astype(jnp.int32), table_slot.astype(jnp.int32))


def route_both(key):
    base_key = jax.random.fold_in(key, 77)
    hot_expert = jax.random.randint(jax.random.fold_in(base_key, 1), (), 0, EXPERTS)
    block_ids = jnp.arange(TOKENS // TOK_DEV, dtype=jnp.int32)
    experts_drawn, slots_drawn = jax.vmap(lambda block_id: route_block(base_key, hot_expert, block_id))(block_ids)
    return (experts_drawn.reshape(TOKENS, TOP), slots_drawn.reshape(TOKENS, TOP))


def draw_route_ids(key, part):
    return route_both(key)[0]


def draw_route_slots(key, part):
    return route_both(key)[1]


def moment_field(key, shape):
    key_rows, key_entries = jax.random.split(key, 2)
    low_scale = 3.0
    high_scale = 30.0
    row_shape = tuple(shape[:-1]) + (1,)
    log_scale = jax.random.uniform(key_rows, row_shape, jnp.float32, jnp.log(low_scale), jnp.log(high_scale))
    entries = jax.random.truncated_normal(key_entries, -4.0, 4.0, tuple(shape), jnp.float32)
    return (jnp.exp(log_scale) * entries).astype(jnp.float32)


def draw_in_moment(key, part):
    return moment_field(jax.random.fold_in(key, 311), (EXPERTS, 2, RANK, D))


def draw_out_moment(key, part):
    return moment_field(jax.random.fold_in(key, 419), (EXPERTS, 2, RANK, FF))


def steps_of(key, shape, cuts, low, largest):
    def one(dim, parts):
        heights = jax.random.uniform(jax.random.fold_in(jax.random.fold_in(key, 6), dim), (parts,), jnp.float32, low / len(cuts), largest / len(cuts))
        return jnp.repeat(jnp.exp(heights), shape[dim] // parts).reshape((-1,) + (1,) * (len(shape) - dim - 1))

    loudness = one(*cuts[0])
    for cut in cuts[1:]:
        loudness = loudness * one(*cut)
    return loudness


def normal_values(own_key, extent, spread, reach, cuts=(), kind=jnp.bfloat16):
    factor_of = steps_of(own_key, extent, cuts, -0.22, 0.18) if cuts else 1.0
    array = jax.random.normal(own_key, extent, jnp.float32) * spread * factor_of
    return jnp.minimum(jnp.maximum(array, -reach), reach).astype(kind)


def setup_inputs(seed: int = 0, part: int = 0) -> dict:
    splits = jax.random.split(jax.random.key(seed), 14)
    own_keys = jax.random.split(jax.random.fold_in(splits[13], part), 14)
    return {
        "tokens": normal_values(own_keys[0], (TOKENS, D), 1.0, 6.0, ((0, 16),)),
        "route_ids": draw_route_ids(jax.random.fold_in(jax.random.fold_in(splits[13], part), 71), part),
        "route_slots": draw_route_slots(jax.random.fold_in(jax.random.fold_in(splits[13], part), 71), part),
        "route_gates": jnp.clip(jnp.exp(math.log(0.35) - 1.9459101 * jax.random.uniform(own_keys[3], (TOKENS, TOP), jnp.float32) ** steps_of(own_keys[3], (TOKENS, TOP), ((0, 16),), -0.2, 0.2)), 0.05, 0.35),
        "out_cotangent": normal_values(own_keys[4], (TOKENS, D), 1.0, 6.0, ((0, 16),)),
        "gate_up_weight": normal_values(splits[5], (EXPERTS, 2, D, FF), D ** -0.5, 0.125, ((0, 8), (3, 2))),
        "w_down": normal_values(splits[6], (EXPERTS, FF, D), FF ** -0.5, 0.21875, ((0, 8), (1, 2))),
        "input_factor": normal_values(splits[7], (EXPERTS, 2, RANK, D), D ** -0.5, 0.125, ((0, 8),), jnp.float32),
        "output_factor": normal_values(splits[8], (EXPERTS, 2, RANK, FF), 0.08, 0.5, ((0, 8), (3, 2)), jnp.float32),
        "gains": jnp.clip(1.0 + 0.1 * jax.random.normal(splits[9], (EXPERTS, 2, FF), jnp.float32), 0.5, 1.5),
        "in_moment": draw_in_moment(jax.random.fold_in(splits[13], 71), part),
        "out_moment": draw_out_moment(jax.random.fold_in(splits[13], 71), part),
        "gain_moment": normal_values(splits[12], (EXPERTS, 2, FF), 0.05, 0.3, ((0, 8), (2, 2)), jnp.float32),
    }


ADAPTER_SCALE = 2.0
MOMENTUM = 0.9
LEARN_RATE = 0.05
NORM_EPS = 1e-06
EXACT_MATMUL = lax.Precision.HIGHEST

def expert_pass(inputs):
    arrived, arrived_grad, frozen_gate_up_pair, down_weight, input_factor, output_factor, gain_pair = inputs
    combined_weight = frozen_gate_up_pair.astype(jnp.float32) + ADAPTER_SCALE * jnp.einsum('qay,qaz->qyz', input_factor, output_factor, precision=EXACT_MATMUL)
    col_norm = jnp.sqrt(lax.optimization_barrier(jnp.sum(combined_weight * combined_weight, axis=1)) + NORM_EPS)
    column_scale_factor = gain_pair / col_norm
    merged = (combined_weight * column_scale_factor[:, None, :]).astype(jnp.bfloat16)
    merged_wide = merged.astype(jnp.float32)
    received_wide_rows = arrived.astype(jnp.float32)
    projected = jnp.einsum('nd,pdf->pnf', received_wide_rows, merged_wide, precision=EXACT_MATMUL)
    gate_pre = projected[0]
    up_pre = projected[1]
    sigmoid_gate = jax.nn.sigmoid(gate_pre)
    hidden = (gate_pre * sigmoid_gate * up_pre).astype(jnp.bfloat16)
    half_width = FF // N_DP
    expert_out = jnp.zeros((arrived.shape[0], D), jnp.float32)
    for index in range(N_DP):
        lower = index * half_width
        term_out = jnp.dot(hidden[:, lower:lower + half_width], down_weight[lower:lower + half_width], preferred_element_type=jnp.float32)
        expert_out = expert_out + lax.optimization_barrier(term_out.astype(jnp.bfloat16)).astype(jnp.float32)
    grad_hidden = jnp.dot(arrived_grad, down_weight.T, preferred_element_type=jnp.float32)
    grad_gate = (grad_hidden * up_pre * sigmoid_gate * (1.0 + gate_pre * (1.0 - sigmoid_gate))).astype(jnp.bfloat16)
    grad_up = (grad_hidden * gate_pre * sigmoid_gate).astype(jnp.bfloat16)
    grad_pair = jnp.stack([grad_gate, grad_up])
    gradient_wide_rows = grad_pair.astype(jnp.float32)
    slot_grad = jnp.zeros((arrived.shape[0], D), jnp.float32)
    for index in range(N_DP):
        lower = index * half_width
        term_grad = jnp.einsum('pnf,pdf->nd', gradient_wide_rows[:, :, lower:lower + half_width], merged_wide[:, :, lower:lower + half_width], precision=EXACT_MATMUL)
        slot_grad = slot_grad + lax.optimization_barrier(term_grad.astype(jnp.bfloat16)).astype(jnp.float32)
    act_sum = lax.optimization_barrier(jnp.sum(gradient_wide_rows * projected, axis=1))
    gain_grad = act_sum / gain_pair
    magnitude_curvature = act_sum / (col_norm * col_norm)
    scaled_out = output_factor * column_scale_factor[:, None, :]
    tilted_weight = output_factor * magnitude_curvature[:, None, :]
    mixed_token_rows = jnp.einsum('pnf,prf->pnr', gradient_wide_rows, scaled_out, precision=EXACT_MATMUL)
    input_factor_gradient = ADAPTER_SCALE * (jnp.einsum('soa,ov->sav', mixed_token_rows, received_wide_rows, precision=EXACT_MATMUL) - jnp.einsum('ujv,uhv->ujh', tilted_weight, combined_weight, precision=EXACT_MATMUL))
    low_rank_rows = jnp.einsum('nd,prd->pnr', received_wide_rows, input_factor, precision=EXACT_MATMUL)
    output_gradient = ADAPTER_SCALE * (jnp.einsum('adl,adm->alm', low_rank_rows, gradient_wide_rows, precision=EXACT_MATMUL) * column_scale_factor[:, None, :] - jnp.einsum('msy,myk->msk', input_factor, combined_weight, precision=EXACT_MATMUL) * magnitude_curvature[:, None, :])
    return (expert_out.astype(jnp.bfloat16), slot_grad.astype(jnp.bfloat16), input_factor_gradient, output_gradient, gain_grad)

def reference(tokens, route_ids, route_slots, route_gates, out_cotangent, gate_up_weight, w_down, input_factor, output_factor, gains, in_moment, out_moment, gain_moment):
    blocks = TOKENS // TOK_DEV
    block_id = (jnp.arange(TOKENS, dtype=jnp.int32) // TOK_DEV).astype(jnp.int32)
    target = ((route_ids * blocks + block_id[:, None]) * CAP + route_slots).astype(jnp.int32)
    flat_target = target.reshape(-1)
    slots_all = EXPERTS * blocks * CAP
    outbound = jnp.zeros((slots_all, D), jnp.bfloat16).at[flat_target].set(jnp.repeat(tokens, TOP, axis=0))
    weighted = (route_gates[:, :, None] * out_cotangent.astype(jnp.float32)[:, None, :]).astype(jnp.bfloat16).reshape(TOKENS * TOP, D)
    grad_outbound = jnp.zeros((slots_all, D), jnp.bfloat16).at[flat_target].set(weighted)
    results = lax.map(expert_pass, (outbound.reshape(EXPERTS, blocks * CAP, D), grad_outbound.reshape(EXPERTS, blocks * CAP, D), gate_up_weight, w_down, input_factor, output_factor, gains))
    expert_out, slot_grad, input_factor_gradient, output_gradient, gain_grad = results
    picked = jnp.take(expert_out.reshape(slots_all, D), flat_target, axis=0).reshape(TOKENS, TOP, D).astype(jnp.float32)
    mixed = lax.optimization_barrier(jnp.sum(picked * route_gates[:, :, None], axis=1)).astype(jnp.bfloat16)
    picked_grad = jnp.take(slot_grad.reshape(slots_all, D), flat_target, axis=0).reshape(TOKENS, TOP, D).astype(jnp.float32)
    token_grad = lax.optimization_barrier(jnp.sum(picked_grad, axis=1)).astype(jnp.bfloat16)
    new_in_moment = MOMENTUM * in_moment + input_factor_gradient
    new_in = input_factor - LEARN_RATE * new_in_moment
    new_out_moment = MOMENTUM * out_moment + output_gradient
    new_out = output_factor - LEARN_RATE * new_out_moment
    new_gain_moment = MOMENTUM * gain_moment + gain_grad
    new_gains = gains - LEARN_RATE * new_gain_moment
    return (mixed, token_grad, new_in, new_in_moment, new_out, new_out_moment, new_gains, new_gain_moment)
```

```python
import functools

import jax
import jax.numpy as jnp
from jax import lax
from jax.experimental import pallas as pl
from jax.experimental.pallas import tpu as pltpu
from jax.sharding import PartitionSpec as P

ADAPTER_SCALE = 2.0
MOMENTUM = 0.9
LEARN_RATE = 0.05
NORM_EPS = 1e-06
BF = jnp.bfloat16
F32 = jnp.float32


MESH = pl.DeviceIdType.MESH


def place():
    e = lax.axis_index("expert")
    return lax.div(e, 2), lax.rem(e, 2), lax.axis_index("dp")


def near(z, y, c, nz):
    return (
        (z < nz - 1, {"expert": (z + 1) * 2 + y}),
        (z > 0, {"expert": (z - 1) * 2 + y}),
        (None, {"expert": z * 2 + 1 - y}),
        (None, {"dp": 1 - c}),
    )


def when(cond, fn):
    if cond is None:
        fn()
    else:
        pl.when(cond)(fn)


def greet(z, y, c, nz):
    barrier = pltpu.get_barrier_semaphore()
    for cond, dev in near(z, y, c, nz):
        when(
            cond,
            lambda dev=dev: pl.semaphore_signal(barrier, 1, device_id=dev, device_id_type=MESH),
        )
    inner = jnp.logical_and(z > 0, z < nz - 1)
    pl.semaphore_wait(barrier, 3 + inner.astype(jnp.int32))


def gather_kernel(
    nz, tok, cot, ids, gates, w, fin, fout, gains, xo, co, go, merged, norm, wide, ssem, rsem
):
    z, y, c = place()
    right, left, across, twin = near(z, y, c, nz)
    outs = (xo, co, go)

    def idx(zz, yy, cc):
        return (zz * 2 + yy) * 2 + cc

    def copy(a, shard, dev, slot):
        return pltpu.make_async_remote_copy(
            src_ref=outs[a].at[shard],
            dst_ref=outs[a].at[shard],
            send_sem=ssem.at[a, slot],
            recv_sem=rsem.at[a, shard],
            device_id=dev,
            device_id_type=MESH,
        )

    def send(shard, dev, slot):
        for a in range(3):
            copy(a, shard, dev, slot).start()

    def got(shard):
        for a in range(3):
            copy(a, shard, twin[1], 0).wait_recv()

    def sent(shard, dev, slot):
        for a in range(3):
            copy(a, shard, dev, slot).wait_send()

    me = idx(z, y, c)
    xo[me] = tok[...]
    co[me] = cot[...]
    rows = tok.shape[0]
    lanes = go.shape[2]
    col = lax.broadcasted_iota(jnp.int32, (rows, lanes), 1)
    dense = jnp.zeros((rows, lanes), F32)
    for k in range(ids.shape[1]):
        dense = dense + jnp.where(col == ids[:, k : k + 1], gates[:, k : k + 1], 0.0)
    go[me] = dense
    greet(z, y, c, nz)

    prep = [(j, p) for j in range(w.shape[0]) for p in range(w.shape[1])]

    def prepare():
        if not prep:
            return
        j, p = prep.pop(0)
        fi = fin[j, p]
        fo = fout[j, p]
        ih = fi.astype(BF)
        il = (fi - ih.astype(F32)).astype(BF)
        oh = fo.astype(BF)
        ol = (fo - oh.astype(F32)).astype(BF)
        lhs = jnp.concatenate([ih, ih, il, il], axis=0)
        rhs = jnp.concatenate([oh, ol, oh, ol], axis=0)
        width = w.shape[2]
        tile = 256
        total = jnp.zeros((1, w.shape[3]), F32)
        for t in range(width // tile):
            low = lax.dot_general(
                lhs[:, t * tile : (t + 1) * tile],
                rhs,
                (((0,), (0,)), ((), ())),
                preferred_element_type=F32,
            )
            part = w[j, p, pl.ds(t * tile, tile), :].astype(F32) + ADAPTER_SCALE * low
            wide[pl.ds(t * tile, tile), :] = part
            total = total + jnp.sum(part * part, axis=0, keepdims=True)
        total = total + NORM_EPS
        norm[j, p] = total
        scale = gains[j, p : p + 1] / jnp.sqrt(total)
        for t in range(width // tile):
            merged[j, p, pl.ds(t * tile, tile), :] = (
                wide[pl.ds(t * tile, tile), :] * scale
            ).astype(BF)

    def step_z(s):
        def from_left():
            shard = idx(z - s, y, c)
            if s:
                got(shard)
            when(right[0], lambda: send(shard, right[1], z - s))
            if not s:
                when(left[0], lambda: send(shard, left[1], nz + z))
            send(shard, across[1], 2 * nz + z - s)
            send(shard, twin[1], 3 * nz + (z - s) * 2 + y)

        def from_right():
            shard = idx(z + s, y, c)
            got(shard)
            when(left[0], lambda: send(shard, left[1], nz + z + s))
            send(shard, across[1], 2 * nz + z + s)
            send(shard, twin[1], 3 * nz + (z + s) * 2 + y)

        if s == 0:
            from_left()
        else:
            pl.when(z - s >= 0)(from_left)
            pl.when(z + s < nz)(from_right)

    def step_y(s):
        def one(zz):
            shard = idx(zz, 1 - y, c)
            got(shard)
            send(shard, twin[1], 3 * nz + zz * 2 + 1 - y)

        if s == 0:
            one(z)
        else:
            pl.when(z - s >= 0)(lambda: one(z - s))
            pl.when(z + s < nz)(lambda: one(z + s))

    step_z(0)
    prepare()
    for s in range(1, nz):
        step_z(s)
        step_y(s - 1)
        prepare()
    step_y(nz - 1)
    while prep:
        prepare()
    for zz in range(nz):
        for yy in range(2):
            got(idx(zz, yy, 1 - c))
    for zz in range(nz):
        here = z >= zz
        pl.when(jnp.logical_and(here, z < nz - 1))(
            lambda: sent(idx(zz, y, c), right[1], zz)
        )
        there = z <= zz
        pl.when(jnp.logical_and(there, z > 0))(
            lambda: sent(idx(zz, y, c), left[1], nz + zz)
        )
        sent(idx(zz, y, c), across[1], 2 * nz + zz)
        for yy in range(2):
            sent(idx(zz, yy, c), twin[1], 3 * nz + zz * 2 + yy)


def scatter_kernel(nz, pa, pb, oa, ob, rd, ys, ry, zs, rz, dss, drs, yss, yrs, zss, zrs):
    z, y, c = place()
    right, left, across, twin = near(z, y, c, nz)
    parts = (pa, pb)
    outs = (oa, ob)

    def idx(zz, yy, cc):
        return (zz * 2 + yy) * 2 + cc

    def remote(src, dst, a, b, dev):
        return pltpu.make_async_remote_copy(
            src_ref=src, dst_ref=dst, send_sem=a, recv_sem=b, device_id=dev, device_id_type=MESH
        )

    def to_twin(m, zz, yy):
        k = zz * 2 + yy
        return remote(
            parts[m].at[idx(zz, yy, 1 - c)], rd.at[m, k], dss.at[m, k], drs.at[m, k], twin[1]
        )

    def to_across(m, zz):
        return remote(ys.at[m, zz], ry.at[m, zz], yss.at[m, zz], yrs.at[m, zz], across[1])

    def to_right(m, zz):
        return remote(
            zs.at[m, zz], rz.at[m, zz + 1], zss.at[m, zz], zrs.at[m, zz + 1], right[1]
        )

    def to_left(m, zz):
        return remote(zs.at[m, zz], rz.at[m, zz], zss.at[m, zz], zrs.at[m, zz], left[1])

    def wide(v):
        return v.astype(F32)

    greet(z, y, c, nz)

    def each(s, fn):
        if s == 0:
            fn(z)
        else:
            pl.when(z + s < nz)(lambda: fn(z + s))
            pl.when(z - s >= 0)(lambda: fn(z - s))

    order = list(range(nz - 1, -1, -1))
    for m in range(2):
        for s in order:
            each(s, lambda zz: to_twin(m, zz, 1 - y).start())
        for s in order:
            each(s, lambda zz: to_twin(m, zz, y).start())

    def y_part(m, s):
        def one(zz):
            to_twin(m, zz, 1 - y).wait_recv()
            ys[m, zz] = (
                wide(parts[m][idx(zz, 1 - y, c)]) + wide(rd[m, zz * 2 + 1 - y])
            ).astype(BF)
            to_across(m, zz).start()

        each(s, one)

    def held(m, zz):
        to_twin(m, zz, y).wait_recv()
        to_across(m, zz).wait_recv()
        return wide(parts[m][idx(zz, y, c)]) + wide(rd[m, zz * 2 + y]) + wide(ry[m, zz])

    def z_part(m, s):
        def rightward():
            zz = z + s
            zs[m, zz] = held(m, zz).astype(BF)

            @pl.when(z > 0)
            def _():
                to_right(m, zz).wait_recv()
                zs[m, zz] = (wide(zs[m, zz]) + wide(rz[m, zz + 1])).astype(BF)

            to_right(m, zz).start()

        def leftward():
            zz = z - s
            zs[m, zz] = held(m, zz).astype(BF)

            @pl.when(z < nz - 1)
            def _():
                to_left(m, zz).wait_recv()
                zs[m, zz] = (wide(zs[m, zz]) + wide(rz[m, zz])).astype(BF)

            to_left(m, zz).start()

        pl.when(z + s < nz)(rightward)
        pl.when(z - s >= 0)(leftward)

    for m in range(2):
        for s in order:
            y_part(m, s)
    for m in range(2):
        for s in order[:-1]:
            z_part(m, s)
        zs[m, z] = held(m, z).astype(BF)

        @pl.when(z > 0)
        def _():
            to_right(m, z).wait_recv()
            zs[m, z] = (wide(zs[m, z]) + wide(rz[m, z + 1])).astype(BF)

        @pl.when(z < nz - 1)
        def _():
            to_left(m, z).wait_recv()
            zs[m, z] = (wide(zs[m, z]) + wide(rz[m, z])).astype(BF)

        outs[m][...] = zs[m, z]
    for m in range(2):
        for zz in range(nz):
            for yy in range(2):
                to_twin(m, zz, yy).wait_send()
            to_across(m, zz).wait_send()
            pl.when(z < zz)(lambda: to_right(m, zz).wait_send())
            pl.when(z > zz)(lambda: to_left(m, zz).wait_send())


def fused_kernel(
    nz, tok, cot, ids, gates, w, wd_in, fin, fout, gains, mom, out_mom, gain_mom,
    mixed, token_grad, new_in, new_mom, new_out, new_out_mom, new_gain, new_gain_mom,
    xg, cg, wv, wd, wdt, cm, cmt, pr, gh, hid, gp, norm, scl, act, inp, rin, rmom, lowt, tt,
    pa, pb, rd, ys, ry, zs, rz,
    lsem, gss, grs, dss, drs, yss, yrs, zss, zrs, ess, ers,
):
    z, y, c = place()
    right, left, across, twin = near(z, y, c, nz)
    parts = (pa, pb)
    outs = (mixed, token_grad)
    rows, width = tok.shape
    nj, _, rank, f = fout.shape
    npair = 2 * nj
    slab = 4 * rows

    def idx(zz, yy, cc):
        return (zz * 2 + yy) * 2 + cc

    def dot(u, v):
        return jnp.dot(u, v, preferred_element_type=F32)

    def dot_nt(u, v):
        return lax.dot_general(u, v, (((1,), (1,)), ((), ())), preferred_element_type=F32)

    def wide(v):
        return v.astype(F32)

    def at(shard):
        return pl.ds(pl.multiple_of(shard * rows, rows), rows)

    def remote(src, dst, a, b, dev):
        return pltpu.make_async_remote_copy(
            src_ref=src, dst_ref=dst, send_sem=a, recv_sem=b, device_id=dev, device_id_type=MESH
        )

    loads = [
        pltpu.make_async_copy(w.at[q // 2, q % 2], wv.at[q], lsem.at[q]) for q in range(npair)
    ]
    load_down = pltpu.make_async_copy(wd_in, wd, lsem.at[npair])
    for load in loads:
        load.start()
    load_down.start()

    me = idx(z, y, c)
    half = (xg.shape[1] - width) // 2
    row = lax.broadcasted_iota(jnp.int32, (half, rows), 0)
    dense = jnp.zeros((half, rows), F32)
    for k in range(ids.shape[0]):
        dense = dense + jnp.where(row == ids[k : k + 1, :], gates[k : k + 1, :], 0.0)
    high = dense.astype(BF)
    both = jnp.concatenate([high, (dense - wide(high)).astype(BF)], axis=0)
    eye = (
        lax.broadcasted_iota(jnp.int32, (rows, rows), 0)
        == lax.broadcasted_iota(jnp.int32, (rows, rows), 1)
    ).astype(BF)
    xg[at(me), pl.ds(0, width)] = tok[...]
    xg[at(me), pl.ds(width, 2 * half)] = dot_nt(eye, both).astype(BF)
    cg[at(me), :] = cot[...]

    held_rows = (xg, cg)

    def gcopy(a, shard, dev, s):
        ref = held_rows[a].at[at(shard), :]
        return remote(ref, ref, gss.at[a, s], grs.at[a, shard], dev)

    def got(a, shard):
        gcopy(a, shard, twin[1], 0).wait_recv()

    def z_step(s, a):
        def from_left():
            shard = idx(z - s, y, c)
            if s:
                got(a, shard)
            when(right[0], lambda: gcopy(a, shard, right[1], z - s).start())
            if not s:
                when(left[0], lambda: gcopy(a, shard, left[1], nz + z).start())
            gcopy(a, shard, across[1], 2 * nz + z - s).start()
            gcopy(a, shard, twin[1], 3 * nz + (z - s) * 2 + y).start()

        def from_right():
            shard = idx(z + s, y, c)
            got(a, shard)
            when(left[0], lambda: gcopy(a, shard, left[1], nz + z + s).start())
            gcopy(a, shard, across[1], 2 * nz + z + s).start()
            gcopy(a, shard, twin[1], 3 * nz + (z + s) * 2 + y).start()

        if s == 0:
            from_left()
        elif s < nz:
            pl.when(z - s >= 0)(from_left)
            pl.when(z + s < nz)(from_right)

    def y_step(s, a):
        def one(zz):
            shard = idx(zz, 1 - y, c)
            got(a, shard)
            gcopy(a, shard, twin[1], 3 * nz + zz * 2 + 1 - y).start()

        if s == 0:
            one(z)
        elif s < nz:
            pl.when(z - s >= 0)(lambda: one(z - s))
            pl.when(z + s < nz)(lambda: one(z + s))

    def slot(k):
        m = jnp.minimum(z, nz - 1 - z)
        close = z - (k + 1) // 2 if k % 2 else z + k // 2
        far = jnp.where(2 * z < nz - 1, z + (k - m), z - (k - m))
        return jnp.where(k <= 2 * m, close, far)

    def to_twin(m, zz, yy):
        k = zz * 2 + yy
        return remote(
            parts[m].at[at(idx(zz, yy, 1 - c)), :], rd.at[m, k], dss.at[m, k], drs.at[m, k], twin[1]
        )

    def to_across(m, zz):
        return remote(ys.at[m, zz], ry.at[m, zz], yss.at[m, zz], yrs.at[m, zz], across[1])

    def to_right(m, zz):
        return remote(
            zs.at[m, zz], rz.at[m, zz + 1], zss.at[m, zz], zrs.at[m, zz + 1], right[1]
        )

    def to_left(m, zz):
        return remote(zs.at[m, zz], rz.at[m, zz], zss.at[m, zz], zrs.at[m, zz], left[1])

    def y_part(m, k):
        zz = slot(k)
        to_twin(m, zz, 1 - y).wait_recv()
        ys[m, zz] = (
            wide(parts[m][at(idx(zz, 1 - y, c)), :]) + wide(rd[m, zz * 2 + 1 - y])
        ).astype(BF)
        to_across(m, zz).start()

    def held(m, zz):
        to_twin(m, zz, y).wait_recv()
        to_across(m, zz).wait_recv()
        return wide(parts[m][at(idx(zz, y, c)), :]) + wide(rd[m, zz * 2 + y]) + wide(ry[m, zz])

    def z_part(m, k):
        zz = slot(k)
        zs[m, zz] = held(m, zz).astype(BF)

        @pl.when(zz > z)
        def _():
            @pl.when(z > 0)
            def _():
                to_right(m, zz).wait_recv()
                zs[m, zz] = (wide(zs[m, zz]) + wide(rz[m, zz + 1])).astype(BF)

            to_right(m, zz).start()

        @pl.when(zz < z)
        def _():
            @pl.when(z < nz - 1)
            def _():
                to_left(m, zz).wait_recv()
                zs[m, zz] = (wide(zs[m, zz]) + wide(rz[m, zz])).astype(BF)

            to_left(m, zz).start()

    def finish(m):
        zs[m, z] = held(m, z).astype(BF)

        @pl.when(z > 0)
        def _():
            to_right(m, z).wait_recv()
            zs[m, z] = (wide(zs[m, z]) + wide(rz[m, z + 1])).astype(BF)

        @pl.when(z < nz - 1)
        def _():
            to_left(m, z).wait_recv()
            zs[m, z] = (wide(zs[m, z]) + wide(rz[m, z])).astype(BF)

        outs[m][...] = zs[m, z]

    def cols(q):
        return pl.ds(q * f, f)

    def prepare(q):
        loads[q].wait()
        fi = fin[q // 2, q % 2]
        fo = fout[q // 2, q % 2]
        ih = fi.astype(BF)
        il = (fi - wide(ih)).astype(BF)
        oh = fo.astype(BF)
        ol = (fo - wide(oh)).astype(BF)
        lhs = jnp.concatenate([ih, ih, il, il], axis=0)
        rhs = jnp.concatenate([oh, ol, oh, ol], axis=0)
        tile = 256
        total = jnp.zeros((8, f), F32)
        for t in range(width // tile):
            low = lax.dot_general(
                lhs[:, t * tile : (t + 1) * tile],
                rhs,
                (((0,), (0,)), ((), ())),
                preferred_element_type=F32,
            )
            part = wide(wv[q, pl.ds(t * tile, tile), :]) + ADAPTER_SCALE * low
            cm[pl.ds(t * tile, tile), cols(q)] = part.astype(BF)
            cmt[cols(q), pl.ds(t * tile, tile)] = part.astype(BF).T
            total = total + jnp.sum((part * part).reshape(tile // 8, 8, f), axis=0)
        total = jnp.sum(total, axis=0, keepdims=True) + NORM_EPS
        norm[q] = total
        scl[q] = gains[q // 2, q % 2 : q % 2 + 1] / jnp.sqrt(total)
        act[q] = jnp.zeros((8, f), F32)

    def turn_down():
        load_down.wait()
        for j in range(nj):
            for t in range(width // 256):
                wdt[pl.ds(t * 256, 256), pl.ds(j * f, f)] = wd[j, :, pl.ds(t * 256, 256)].T

    start = lax.axis_index("expert") * nj
    tile = 32
    lane = lax.broadcasted_iota(jnp.int32, (tile, 2 * half), 1)

    def gate_of(r, j):
        g = wide(xg[r, pl.ds(width, 2 * half)])
        mine = (lane == start + j) | (lane == start + j + half)
        return jnp.sum(jnp.where(mine, g, 0.0), axis=1, keepdims=True)

    def forward(k):
        zz = slot(k)
        base = zz * slab
        r = pl.ds(pl.multiple_of(base, slab), slab)
        for yy in range(2):
            got(0, idx(zz, yy, 1 - c))
        for j in range(nj):
            n = pl.ds(j * 2 * f, 2 * f)
            pr[r, n] = dot(xg[r, pl.ds(0, width)], cm[:, n])

        def gating(i, _):
            t = pl.ds(pl.multiple_of(base + i * tile, tile), tile)
            here = pl.ds(pl.multiple_of(i * tile, tile), tile)
            for j in range(nj):
                pre = pr[t, cols(2 * j)] * scl[2 * j]
                up = pr[t, cols(2 * j + 1)] * scl[2 * j + 1]
                hid[here, cols(j)] = (pre * jax.nn.sigmoid(pre) * up * gate_of(t, j)).astype(BF)
            return 0

        lax.fori_loop(0, slab // tile, gating, 0)
        for t in range(width // 512):
            n = pl.ds(t * 512, 512)
            acc = dot(hid[:, cols(0)], wd[0, :, n])
            for j in range(1, nj):
                acc = acc + dot(hid[:, cols(j)], wd[j, :, n])
            pa[r, n] = acc.astype(BF)
        for yy in range(2):
            to_twin(0, zz, yy).start()

    def backward(k):
        zz = slot(k)
        base = zz * slab
        r = pl.ds(pl.multiple_of(base, slab), slab)
        for yy in range(2):
            got(1, idx(zz, yy, 1 - c))
        gh[...] = dot(cg[r, :], wdt[...])

        def gating(i, _):
            t = pl.ds(pl.multiple_of(base + i * tile, tile), tile)
            here = pl.ds(pl.multiple_of(i * tile, tile), tile)
            for j in range(nj):
                raw0 = pr[t, cols(2 * j)]
                raw1 = pr[t, cols(2 * j + 1)]
                s0 = scl[2 * j]
                s1 = scl[2 * j + 1]
                pre = raw0 * s0
                up = raw1 * s1
                s = jax.nn.sigmoid(pre)
                gr = gh[here, cols(j)] * gate_of(t, j)
                g0 = (gr * up * s * (1.0 + pre * (1.0 - s)) * s0).astype(BF)
                g1 = (gr * pre * s * s1).astype(BF)
                gp[t, cols(2 * j)] = g0
                gp[t, cols(2 * j + 1)] = g1
                for q, g, raw in ((2 * j, g0, raw0), (2 * j + 1, g1, raw1)):
                    term = wide(g) * raw
                    act[q] += jnp.sum(term.reshape(tile // 8, 8, f), axis=0)
            return 0

        lax.fori_loop(0, slab // tile, gating, 0)
        for t in range(width // 512):
            n = pl.ds(t * 512, 512)
            acc = dot(gp[r, pl.ds(0, 2 * f)], cmt[pl.ds(0, 2 * f), n])
            for j in range(1, nj):
                k2 = pl.ds(j * 2 * f, 2 * f)
                acc = acc + dot(gp[r, k2], cmt[k2, n])
            pb[r, n] = acc.astype(BF)
        for yy in range(2):
            to_twin(1, zz, yy).start()

    group = [pl.ds(q * rank, rank) for q in range(npair)]

    def low_in():
        ih = jnp.concatenate([fin[q // 2, q % 2] for q in range(npair)], axis=0).astype(BF)
        lowt[...] = dot_nt(ih, xg[:, pl.ds(0, width)])

    def low_out():
        for q in range(npair):
            tt[group[q], :] = dot_nt(fout[q // 2, q % 2].astype(BF), gp[:, cols(q)])
        inp[...] = dot(tt[...].astype(BF), xg[:, pl.ds(0, width)])

    def total_act(q):
        return jnp.sum(act[q], axis=0, keepdims=True)

    def in_part():
        for q in range(npair):
            curved = fout[q // 2, q % 2] * (total_act(q) / norm[q])
            low = dot(curved.astype(BF), cmt[cols(q), :])
            inp[group[q], :] = ADAPTER_SCALE * (inp[group[q], :] - low)
        swap_inp.start()

    def out_part(q):
        j, p = q // 2, q % 2
        total = total_act(q)
        first = dot(lowt[group[q], :].astype(BF), gp[:, cols(q)])
        second = dot(fin[j, p].astype(BF), cm[:, cols(q)]) * (total / norm[q])
        moved = MOMENTUM * out_mom[j, p] + ADAPTER_SCALE * (first - second)
        new_out_mom[j, p] = moved
        new_out[j, p] = fout[j, p] - LEARN_RATE * moved
        one = pl.ds(p, 1)
        bent = MOMENTUM * gain_mom[j, one, :] + total / gains[j, one, :]
        new_gain_mom[j, one, :] = bent
        new_gain[j, one, :] = gains[j, one, :] - LEARN_RATE * bent

    def in_finish():
        swap_mom.wait()
        swap_inp.wait()
        share = mom.shape[1]
        for own in range(2):
            k = pl.ds(pl.multiple_of((c if own else 1 - c) * share, share), share)
            old = mom[...] if own else rmom[...]
            moved = MOMENTUM * old + (inp[:, k] + rin[:, k])
            if own:
                new_mom[...] = moved
            for q in range(npair):
                new_in[q // 2, q % 2, :, k] = (
                    fin[q // 2, q % 2, :, k]
                    - LEARN_RATE * moved[q * rank : (q + 1) * rank]
                )

    swap_mom = remote(mom, rmom, ess.at[0], ers.at[0], twin[1])
    swap_inp = remote(inp, rin, ess.at[1], ers.at[1], twin[1])

    greet(z, y, c, nz)
    z_step(0, 0)
    for q in range(npair):
        prepare(q)
        if q == npair // 2 - 1:
            z_step(1, 0)
    for k in range(nz):
        y_step(k, 0)
        if k == 0:
            turn_down()
        forward(k)
        z_step(k + 2, 0)
        z_step(k, 1)
        if k == 0:
            swap_mom.start()
        if k >= 2:
            y_step(k - 2, 1)
    y_part(0, nz - 1)
    for k in range(nz):
        backward(k)
        y_step(k + max(nz - 2, 0), 1)
        if k + 1 < nz:
            y_part(0, nz - 2 - k)
    for k in range(nz - 1, -1, -1):
        y_part(1, k)
    fillers = [low_in, low_out, in_part] + [functools.partial(out_part, q) for q in range(npair)]
    for m in range(2):
        for k in range(nz - 1, 0, -1):
            z_part(m, k)
            if fillers:
                fillers.pop(0)()
        finish(m)
        if fillers:
            fillers.pop(0)()
    while fillers:
        fillers.pop(0)()
    in_finish()
    for a in range(2):
        for zz in range(nz):
            pl.when(jnp.logical_and(z >= zz, z < nz - 1))(
                lambda: gcopy(a, idx(zz, y, c), right[1], zz).wait_send()
            )
            pl.when(jnp.logical_and(z <= zz, z > 0))(
                lambda: gcopy(a, idx(zz, y, c), left[1], nz + zz).wait_send()
            )
            gcopy(a, idx(zz, y, c), across[1], 2 * nz + zz).wait_send()
            for yy in range(2):
                gcopy(a, idx(zz, yy, c), twin[1], 3 * nz + zz * 2 + yy).wait_send()
    for m in range(2):
        for zz in range(nz):
            for yy in range(2):
                to_twin(m, zz, yy).wait_send()
            to_across(m, zz).wait_send()
            pl.when(z < zz)(lambda: to_right(m, zz).wait_send())
            pl.when(z > zz)(lambda: to_left(m, zz).wait_send())


def place_kernel(*refs):
    n = (len(refs) - 1) // 2
    sems = refs[-1]
    moves = [
        pltpu.make_async_copy(refs[k], refs[n + k], sems.at[k]) for k in range(n)
    ]
    for move in moves:
        move.start()
    for move in moves:
        move.wait()


VM = pl.BlockSpec(memory_space=pltpu.VMEM)
HBM = pl.BlockSpec(memory_space=pl.ANY)
DMA = pltpu.SemaphoreType.DMA


def gather(nz, tok, cot, ids, gates, w, fin, fout, gains, lanes):
    n = nz * 4
    rows, width = tok.shape
    j, p, d, f = w.shape
    return pl.pallas_call(
        functools.partial(gather_kernel, nz),
        out_shape=(
            jax.ShapeDtypeStruct((n, rows, width), BF),
            jax.ShapeDtypeStruct((n, rows, width), BF),
            jax.ShapeDtypeStruct((n, rows, lanes), F32),
            jax.ShapeDtypeStruct(w.shape, BF),
            jax.ShapeDtypeStruct((j, p, 1, f), F32),
        ),
        in_specs=[VM] * 8,
        out_specs=[VM] * 5,
        scratch_shapes=[pltpu.VMEM((d, f), F32), DMA((3, 5 * nz)), DMA((3, n))],
        compiler_params=pltpu.CompilerParams(
            collective_id=0, has_side_effects=True, vmem_limit_bytes=56 << 20
        ),
    )(tok, cot, ids, gates, w, fin, fout, gains)


def scatter(nz, pa, pb):
    n, rows, width = pa.shape
    row = jax.ShapeDtypeStruct((rows, width), BF)
    return pl.pallas_call(
        functools.partial(scatter_kernel, nz),
        out_shape=(row, row),
        in_specs=[VM] * 2,
        out_specs=[VM] * 2,
        scratch_shapes=[
            pltpu.VMEM((2, nz * 2, rows, width), BF),
            pltpu.VMEM((2, nz, rows, width), BF),
            pltpu.VMEM((2, nz, rows, width), BF),
            pltpu.VMEM((2, nz, rows, width), BF),
            pltpu.VMEM((2, nz + 1, rows, width), BF),
            DMA((2, nz * 2)),
            DMA((2, nz * 2)),
            DMA((2, nz)),
            DMA((2, nz)),
            DMA((2, nz)),
            DMA((2, nz + 1)),
        ],
        compiler_params=pltpu.CompilerParams(
            collective_id=1, has_side_effects=True, vmem_limit_bytes=56 << 20
        ),
    )(pa, pb)


def fused(nz, tok, cot, ids, gates, w, wd, fin, fout, gains, mom, out_mom, gain_mom):
    rows, width = tok.shape
    n = 4 * nz
    n_tok = n * rows
    nj, _, rank, f = fout.shape
    q = 2 * nj
    VMEM = pltpu.VMEM
    shape = jax.ShapeDtypeStruct
    row = shape((rows, width), BF)
    results = (
        row,
        row,
        shape(fin.shape, F32),
        shape(mom.shape, F32),
        shape(fout.shape, F32),
        shape(fout.shape, F32),
        shape(gains.shape, F32),
        shape(gains.shape, F32),
    )
    made = pl.pallas_call(
        functools.partial(fused_kernel, nz),
        out_shape=results,
        in_specs=[VM] * 4 + [HBM] * 2 + [VM] * 6,
        out_specs=[VM] * 8,
        scratch_shapes=[
            VMEM((n_tok, width + 128), BF),
            VMEM((n_tok, width), BF),
            VMEM((q, width, f), BF),
            VMEM((nj, f, width), BF),
            VMEM((width, nj * f), BF),
            VMEM((width, q * f), BF),
            VMEM((q * f, width), BF),
            VMEM((n_tok, q * f), F32),
            VMEM((4 * rows, nj * f), F32),
            VMEM((4 * rows, nj * f), BF),
            VMEM((n_tok, q * f), BF),
            VMEM((q, 1, f), F32),
            VMEM((q, 1, f), F32),
            VMEM((q, 8, f), F32),
            VMEM((q * rank, width), F32),
            VMEM((q * rank, width), F32),
            VMEM(mom.shape, F32),
            VMEM((q * rank, n_tok), F32),
            VMEM((q * rank, n_tok), F32),
            VMEM((n_tok, width), BF),
            VMEM((n_tok, width), BF),
            VMEM((2, nz * 2, rows, width), BF),
            VMEM((2, nz, rows, width), BF),
            VMEM((2, nz, rows, width), BF),
            VMEM((2, nz, rows, width), BF),
            VMEM((2, nz + 1, rows, width), BF),
            DMA((q + 1,)),
            DMA((2, 5 * nz)),
            DMA((2, n)),
            DMA((2, nz * 2)),
            DMA((2, nz * 2)),
            DMA((2, nz)),
            DMA((2, nz)),
            DMA((2, nz)),
            DMA((2, nz + 1)),
            DMA((2,)),
            DMA((2,)),
        ],
        compiler_params=pltpu.CompilerParams(
            collective_id=2, has_side_effects=True, vmem_limit_bytes=58 << 20
        ),
    )(tok, cot, ids, gates, w, wd, fin, fout, gains, mom, out_mom, gain_mom)
    return pl.pallas_call(
        place_kernel,
        out_shape=results,
        in_specs=[HBM] * 8,
        out_specs=[HBM] * 8,
        scratch_shapes=[DMA((8,))],
    )(*made)


def mm(spec, a, b):
    return jnp.einsum(spec, a, b, preferred_element_type=F32)


def update(
    new_mom_all, out_grad, gain_grad, input_factor, output_factor, gains,
    in_moment, out_moment, gain_moment,
):
    new_in = input_factor - LEARN_RATE * new_mom_all
    share = in_moment.shape[3]
    new_in_moment = lax.dynamic_slice_in_dim(new_mom_all, lax.axis_index("dp") * share, share, 3)
    new_out_moment = MOMENTUM * out_moment + out_grad
    new_out = output_factor - LEARN_RATE * new_out_moment
    new_gain_moment = MOMENTUM * gain_moment + gain_grad
    new_gains = gains - LEARN_RATE * new_gain_moment
    return new_in, new_in_moment, new_out, new_out_moment, new_gains, new_gain_moment


def body(
    tokens,
    route_ids,
    route_slots,
    route_gates,
    out_cotangent,
    gate_up_weight,
    w_down,
    input_factor,
    output_factor,
    gains,
    in_moment,
    out_moment,
    gain_moment,
):
    n_expert = lax.axis_size("expert")
    experts_here = w_down.shape[0]
    experts_all = experts_here * n_expert
    tok_here, width = tokens.shape
    nz = n_expert // 2
    lanes = -(-experts_all // 128) * 128
    n_all = 4 * nz * tok_here
    if n_all <= 1024 and experts_all <= 64:
        share = in_moment.shape[3]
        mixed, token_grad, new_in, new_mom, *rest = fused(
            nz, tokens, out_cotangent, route_ids.T, route_gates.T, gate_up_weight, w_down,
            input_factor, output_factor, gains, in_moment.reshape(-1, share), out_moment,
            gain_moment,
        )
        return (mixed, token_grad, new_in, new_mom.reshape(in_moment.shape), *rest)
    x, c, g, merged, norm2 = gather(
        nz, tokens, out_cotangent, route_ids, route_gates, gate_up_weight,
        input_factor, output_factor, gains, lanes,
    )
    x = x.reshape(n_all, width)
    c = c.reshape(n_all, width)
    moment_all = lax.all_gather(in_moment, "dp", axis=3, tiled=True)
    norm2 = norm2[:, :, 0]
    col_norm = jnp.sqrt(norm2)
    col_scale = gains / col_norm
    moment_all = lax.all_gather(in_moment, "dp", axis=3, tiled=True)

    i_hi = input_factor.astype(BF)
    start = lax.axis_index("expert") * experts_here
    gate = lax.dynamic_slice_in_dim(g.reshape(n_all, lanes), start, experts_here, 1)
    gate = gate.T[:, :, None]

    projected = mm("td,jpdf->jptf", x, merged)
    gate_pre = projected[:, 0]
    up_pre = projected[:, 1]
    s = jax.nn.sigmoid(gate_pre)
    hidden = (gate_pre * s * up_pre * gate).astype(BF)
    grad_hidden = mm("td,jfd->jtf", c, w_down) * gate
    grad_gate = (grad_hidden * up_pre * s * (1.0 + gate_pre * (1.0 - s))).astype(BF)
    grad_up = (grad_hidden * gate_pre * s).astype(BF)
    grad_pair = jnp.stack([grad_gate, grad_up], axis=1)
    part_mixed = mm("jtf,jfd->td", hidden, w_down).astype(BF)
    part_grad = mm("jptf,jpdf->td", grad_pair, merged).astype(BF)
    split = (4 * nz, tok_here, width)
    mixed, token_grad = scatter(nz, part_mixed.reshape(split), part_grad.reshape(split))

    act_sum = jnp.sum(grad_pair.astype(F32) * projected, axis=2)
    gain_grad = act_sum / gains
    curvature = act_sum / norm2
    scaled_out = output_factor * col_scale[:, :, None, :]
    tilted = output_factor * (curvature / col_scale)[:, :, None, :]
    t_rows = mm("jptf,jprf->jptr", grad_pair, scaled_out.astype(BF))
    in_part = ADAPTER_SCALE * (
        mm("jptr,td->jprd", t_rows.astype(BF), x)
        - mm("jprf,jpdf->jprd", tilted.astype(BF), merged)
    )
    low_rows = mm("td,jprd->jptr", x, i_hi)
    out_grad = ADAPTER_SCALE * (
        mm("jptr,jptf->jprf", low_rows.astype(BF), grad_pair) * col_scale[:, :, None, :]
        - mm("jprd,jpdf->jprf", i_hi, merged) * (curvature / col_scale)[:, :, None, :]
    )
    n_dp = lax.axis_size("dp")
    mine = in_part
    pieces = lax.all_gather(mine, "dp", axis=0)
    in_grad = pieces[0]
    for k in range(1, n_dp):
        in_grad = in_grad + pieces[k]
    new_mom_all = MOMENTUM * moment_all + in_grad
    return (mixed, token_grad) + update(
        new_mom_all, out_grad, gain_grad, input_factor, output_factor, gains,
        in_moment, out_moment, gain_moment,
    )


def solution(mesh):
    return jax.shard_map(
        body,
        mesh=mesh,
        in_specs=(
            P(("groups", "expert", "dp"), None),
            P(("groups", "expert", "dp"), None),
            P(("groups", "expert", "dp"), None),
            P(("groups", "expert", "dp"), None),
            P(("groups", "expert", "dp"), None),
            P("expert", None, None, "dp"),
            P("expert", "dp", None),
            P("expert", None, None, None),
            P("expert", None, None, "dp"),
            P("expert", None, "dp"),
            P("expert", None, None, "dp"),
            P("expert", None, None, "dp"),
            P("expert", None, "dp"),
        ),
        out_specs=(
            P(("groups", "expert", "dp"), None),
            P(("groups", "expert", "dp"), None),
            P(("groups", "expert"), None, None, None),
            P(("groups", "expert"), None, None, "dp"),
            P(("groups", "expert"), None, None, "dp"),
            P(("groups", "expert"), None, None, "dp"),
            P(("groups", "expert"), None, "dp"),
            P(("groups", "expert"), None, "dp"),
        ),
        check_vma=False,
    )
```

```python
import functools

import jax
import jax.numpy as jnp
from jax import lax
from jax.experimental import pallas as pl
from jax.experimental.pallas import tpu as pltpu
from jax.sharding import PartitionSpec as P

ADAPTER_SCALE = 2.0
MOMENTUM = 0.9
LEARN_RATE = 0.05
NORM_EPS = 1e-06
BF = jnp.bfloat16
F32 = jnp.float32


MESH = pl.DeviceIdType.MESH


def place():
    e = lax.axis_index("expert")
    return lax.div(e, 2), lax.rem(e, 2), lax.axis_index("dp")


def near(z, y, c, nz):
    return (
        (z < nz - 1, {"expert": (z + 1) * 2 + y}),
        (z > 0, {"expert": (z - 1) * 2 + y}),
        (None, {"expert": z * 2 + 1 - y}),
        (None, {"dp": 1 - c}),
    )


def when(cond, fn):
    if cond is None:
        fn()
    else:
        pl.when(cond)(fn)


def hail(z, y, c, nz):
    barrier = pltpu.get_barrier_semaphore()
    for cond, dev in near(z, y, c, nz):
        when(
            cond,
            lambda dev=dev: pl.semaphore_signal(barrier, 1, device_id=dev, device_id_type=MESH),
        )
    inner = jnp.logical_and(z > 0, z < nz - 1)
    return lambda: pl.semaphore_wait(barrier, 3 + inner.astype(jnp.int32))


def greet(z, y, c, nz):
    hail(z, y, c, nz)()


def gather_kernel(
    nz, tok, cot, ids, gates, w, fin, fout, gains, xo, co, go, merged, norm, wide, ssem, rsem
):
    z, y, c = place()
    right, left, across, twin = near(z, y, c, nz)
    outs = (xo, co, go)

    def idx(zz, yy, cc):
        return (zz * 2 + yy) * 2 + cc

    def copy(a, shard, dev, slot):
        return pltpu.make_async_remote_copy(
            src_ref=outs[a].at[shard],
            dst_ref=outs[a].at[shard],
            send_sem=ssem.at[a, slot],
            recv_sem=rsem.at[a, shard],
            device_id=dev,
            device_id_type=MESH,
        )

    def send(shard, dev, slot):
        for a in range(3):
            copy(a, shard, dev, slot).start()

    def got(shard):
        for a in range(3):
            copy(a, shard, twin[1], 0).wait_recv()

    def sent(shard, dev, slot):
        for a in range(3):
            copy(a, shard, dev, slot).wait_send()

    me = idx(z, y, c)
    xo[me] = tok[...]
    co[me] = cot[...]
    rows = tok.shape[0]
    lanes = go.shape[2]
    col = lax.broadcasted_iota(jnp.int32, (rows, lanes), 1)
    dense = jnp.zeros((rows, lanes), F32)
    for k in range(ids.shape[1]):
        dense = dense + jnp.where(col == ids[:, k : k + 1], gates[:, k : k + 1], 0.0)
    go[me] = dense
    greet(z, y, c, nz)

    prep = [(j, p) for j in range(w.shape[0]) for p in range(w.shape[1])]

    def prepare():
        if not prep:
            return
        j, p = prep.pop(0)
        fi = fin[j, p]
        fo = fout[j, p]
        ih = fi.astype(BF)
        il = (fi - ih.astype(F32)).astype(BF)
        oh = fo.astype(BF)
        ol = (fo - oh.astype(F32)).astype(BF)
        lhs = jnp.concatenate([ih, ih, il, il], axis=0)
        rhs = jnp.concatenate([oh, ol, oh, ol], axis=0)
        width = w.shape[2]
        tile = 256
        total = jnp.zeros((1, w.shape[3]), F32)
        for t in range(width // tile):
            low = lax.dot_general(
                lhs[:, t * tile : (t + 1) * tile],
                rhs,
                (((0,), (0,)), ((), ())),
                preferred_element_type=F32,
            )
            part = w[j, p, pl.ds(t * tile, tile), :].astype(F32) + ADAPTER_SCALE * low
            wide[pl.ds(t * tile, tile), :] = part
            total = total + jnp.sum(part * part, axis=0, keepdims=True)
        total = total + NORM_EPS
        norm[j, p] = total
        scale = gains[j, p : p + 1] / jnp.sqrt(total)
        for t in range(width // tile):
            merged[j, p, pl.ds(t * tile, tile), :] = (
                wide[pl.ds(t * tile, tile), :] * scale
            ).astype(BF)

    def step_z(s):
        def from_left():
            shard = idx(z - s, y, c)
            if s:
                got(shard)
            when(right[0], lambda: send(shard, right[1], z - s))
            if not s:
                when(left[0], lambda: send(shard, left[1], nz + z))
            send(shard, across[1], 2 * nz + z - s)
            send(shard, twin[1], 3 * nz + (z - s) * 2 + y)

        def from_right():
            shard = idx(z + s, y, c)
            got(shard)
            when(left[0], lambda: send(shard, left[1], nz + z + s))
            send(shard, across[1], 2 * nz + z + s)
            send(shard, twin[1], 3 * nz + (z + s) * 2 + y)

        if s == 0:
            from_left()
        else:
            pl.when(z - s >= 0)(from_left)
            pl.when(z + s < nz)(from_right)

    def step_y(s):
        def one(zz):
            shard = idx(zz, 1 - y, c)
            got(shard)
            send(shard, twin[1], 3 * nz + zz * 2 + 1 - y)

        if s == 0:
            one(z)
        else:
            pl.when(z - s >= 0)(lambda: one(z - s))
            pl.when(z + s < nz)(lambda: one(z + s))

    step_z(0)
    prepare()
    for s in range(1, nz):
        step_z(s)
        step_y(s - 1)
        prepare()
    step_y(nz - 1)
    while prep:
        prepare()
    for zz in range(nz):
        for yy in range(2):
            got(idx(zz, yy, 1 - c))
    for zz in range(nz):
        here = z >= zz
        pl.when(jnp.logical_and(here, z < nz - 1))(
            lambda: sent(idx(zz, y, c), right[1], zz)
        )
        there = z <= zz
        pl.when(jnp.logical_and(there, z > 0))(
            lambda: sent(idx(zz, y, c), left[1], nz + zz)
        )
        sent(idx(zz, y, c), across[1], 2 * nz + zz)
        for yy in range(2):
            sent(idx(zz, yy, c), twin[1], 3 * nz + zz * 2 + yy)


def scatter_kernel(nz, pa, pb, oa, ob, rd, ys, ry, zs, rz, dss, drs, yss, yrs, zss, zrs):
    z, y, c = place()
    right, left, across, twin = near(z, y, c, nz)
    parts = (pa, pb)
    outs = (oa, ob)

    def idx(zz, yy, cc):
        return (zz * 2 + yy) * 2 + cc

    def remote(src, dst, a, b, dev):
        return pltpu.make_async_remote_copy(
            src_ref=src, dst_ref=dst, send_sem=a, recv_sem=b, device_id=dev, device_id_type=MESH
        )

    def to_twin(m, zz, yy):
        k = zz * 2 + yy
        return remote(
            parts[m].at[idx(zz, yy, 1 - c)], rd.at[m, k], dss.at[m, k], drs.at[m, k], twin[1]
        )

    def to_across(m, zz):
        return remote(ys.at[m, zz], ry.at[m, zz], yss.at[m, zz], yrs.at[m, zz], across[1])

    def to_right(m, zz):
        return remote(
            zs.at[m, zz], rz.at[m, zz + 1], zss.at[m, zz], zrs.at[m, zz + 1], right[1]
        )

    def to_left(m, zz):
        return remote(zs.at[m, zz], rz.at[m, zz], zss.at[m, zz], zrs.at[m, zz], left[1])

    def wide(v):
        return v.astype(F32)

    greet(z, y, c, nz)

    def each(s, fn):
        if s == 0:
            fn(z)
        else:
            pl.when(z + s < nz)(lambda: fn(z + s))
            pl.when(z - s >= 0)(lambda: fn(z - s))

    order = list(range(nz - 1, -1, -1))
    for m in range(2):
        for s in order:
            each(s, lambda zz: to_twin(m, zz, 1 - y).start())
        for s in order:
            each(s, lambda zz: to_twin(m, zz, y).start())

    def y_part(m, s):
        def one(zz):
            to_twin(m, zz, 1 - y).wait_recv()
            ys[m, zz] = (
                wide(parts[m][idx(zz, 1 - y, c)]) + wide(rd[m, zz * 2 + 1 - y])
            ).astype(BF)
            to_across(m, zz).start()

        each(s, one)

    def held(m, zz):
        to_twin(m, zz, y).wait_recv()
        to_across(m, zz).wait_recv()
        return wide(parts[m][idx(zz, y, c)]) + wide(rd[m, zz * 2 + y]) + wide(ry[m, zz])

    def z_part(m, s):
        def rightward():
            zz = z + s
            zs[m, zz] = held(m, zz).astype(BF)

            @pl.when(z > 0)
            def _():
                to_right(m, zz).wait_recv()
                zs[m, zz] = (wide(zs[m, zz]) + wide(rz[m, zz + 1])).astype(BF)

            to_right(m, zz).start()

        def leftward():
            zz = z - s
            zs[m, zz] = held(m, zz).astype(BF)

            @pl.when(z < nz - 1)
            def _():
                to_left(m, zz).wait_recv()
                zs[m, zz] = (wide(zs[m, zz]) + wide(rz[m, zz])).astype(BF)

            to_left(m, zz).start()

        pl.when(z + s < nz)(rightward)
        pl.when(z - s >= 0)(leftward)

    for m in range(2):
        for s in order:
            y_part(m, s)
    for m in range(2):
        for s in order[:-1]:
            z_part(m, s)
        zs[m, z] = held(m, z).astype(BF)

        @pl.when(z > 0)
        def _():
            to_right(m, z).wait_recv()
            zs[m, z] = (wide(zs[m, z]) + wide(rz[m, z + 1])).astype(BF)

        @pl.when(z < nz - 1)
        def _():
            to_left(m, z).wait_recv()
            zs[m, z] = (wide(zs[m, z]) + wide(rz[m, z])).astype(BF)

        outs[m][...] = zs[m, z]
    for m in range(2):
        for zz in range(nz):
            for yy in range(2):
                to_twin(m, zz, yy).wait_send()
            to_across(m, zz).wait_send()
            pl.when(z < zz)(lambda: to_right(m, zz).wait_send())
            pl.when(z > zz)(lambda: to_left(m, zz).wait_send())


GATHER_BYPASS = (False, True)
SCATTER_BYPASS = (False, False)
PLAN_NZ = 4
PLAN = (
    ("z", 0, 0), ("z", 5, 0), ("p", 3), ("p", 0), ("z", 0, 1), ("p", 2), ("p", 1), ("t",),
    ("y", 0, 0), ("z", 1, 0), ("z", 1, 1), ("y", 0, 1), ("U", 0), ("D", 0), ("z", 2, 0),
    ("y", 1, 0), ("U", 1), ("z", 2, 1), ("D", 1), ("z", 4, 0), ("V", 0), ("Y", 0, 1), ("W", 0),
    ("y", 2, 0), ("z", 3, 0), ("y", 1, 1), ("V", 1), ("z", 3, 1), ("Y", 1, 0), ("U", 2),
    ("y", 3, 0), ("U", 3), ("y", 2, 1), ("D", 2), ("D", 3), ("Y", 0, 3), ("y", 3, 1), ("V", 3),
    ("Y", 0, 2), ("V", 2), ("W", 1), ("Z", 0, 3), ("W", 3), ("Y", 1, 3), ("W", 2), ("m",),
    ("Y", 1, 1), ("Z", 0, 2), ("x",), ("Z", 1, 3), ("Y", 1, 2), ("Y", 0, 0), ("x",),
    ("Z", 0, 1), ("x",), ("Z", 1, 2), ("Z", 1, 1), ("x",), ("x",), ("x",), ("E", 0), ("x",),
    ("E", 1),
)


def fused_kernel(
    nz, tok, cot, ids, gates, w, wd_in, fin, fout, gains, mom, out_mom, gain_mom,
    mixed, token_grad, new_in, new_mom, new_out, new_out_mom, new_gain, new_gain_mom,
    xg, cg, wv, wd, wdt, cm, cmt, pr, gh, hid, gp, norm, scl, act, inp, rin, rmom, lowt, tt,
    pa, pb, rd, ys, ry, zs, rz,
    lsem, gss, grs, dss, drs, yss, yrs, zss, zrs, ess, ers, pss, prs, rp,
):
    z, y, c = place()
    right, left, across, twin = near(z, y, c, nz)
    pz = z + 1 - 2 * lax.rem(z, 2)
    partner = {"expert": pz * 2 + y}
    heard = hail(z, y, c, nz)
    parts = (pa, pb)
    outs = (mixed, token_grad)
    rows, width = tok.shape
    nj, _, rank, f = fout.shape
    npair = 2 * nj
    slab = 4 * rows

    def idx(zz, yy, cc):
        return (zz * 2 + yy) * 2 + cc

    def dot(u, v):
        return jnp.dot(u, v, preferred_element_type=F32)

    def dot_nt(u, v):
        return lax.dot_general(u, v, (((1,), (1,)), ((), ())), preferred_element_type=F32)

    def wide(v):
        return v.astype(F32)

    def at(shard):
        return pl.ds(pl.multiple_of(shard * rows, rows), rows)

    def remote(src, dst, a, b, dev):
        return pltpu.make_async_remote_copy(
            src_ref=src, dst_ref=dst, send_sem=a, recv_sem=b, device_id=dev, device_id_type=MESH
        )

    loads = [
        pltpu.make_async_copy(w.at[q // 2, q % 2], wv.at[q], lsem.at[q]) for q in range(npair)
    ]
    load_down = pltpu.make_async_copy(wd_in, wd, lsem.at[npair])
    for load in loads:
        load.start()
    load_down.start()

    me = idx(z, y, c)
    half = (xg.shape[1] - width) // 2
    row = lax.broadcasted_iota(jnp.int32, (half, rows), 0)
    dense = jnp.zeros((half, rows), F32)
    for k in range(ids.shape[0]):
        dense = dense + jnp.where(row == ids[k : k + 1, :], gates[k : k + 1, :], 0.0)
    high = dense.astype(BF)
    both = jnp.concatenate([high, (dense - wide(high)).astype(BF)], axis=0)
    eye = (
        lax.broadcasted_iota(jnp.int32, (rows, rows), 0)
        == lax.broadcasted_iota(jnp.int32, (rows, rows), 1)
    ).astype(BF)
    xg[at(me), pl.ds(0, width)] = tok[...]
    xg[at(me), pl.ds(width, 2 * half)] = dot_nt(eye, both).astype(BF)
    cg[at(me), :] = cot[...]

    held_rows = (xg, cg)

    def gcopy(a, shard, dev, s):
        ref = held_rows[a].at[at(shard), :]
        return remote(ref, ref, gss.at[a, s], grs.at[a, shard], dev)

    def got(a, shard):
        gcopy(a, shard, twin[1], 0).wait_recv()

    def cross(a, s, zz):
        send = gcopy(a, idx(zz, y, c), across[1], 2 * nz + zz)
        if GATHER_BYPASS[a] and s == 1:
            pl.when(zz != pz)(lambda: send.start())
        else:
            send.start()

    def z_step(s, a):
        def from_left():
            shard = idx(z - s, y, c)
            if s:
                got(a, shard)
            when(right[0], lambda: gcopy(a, shard, right[1], z - s).start())
            if not s:
                when(left[0], lambda: gcopy(a, shard, left[1], nz + z).start())
            cross(a, s, z - s)
            gcopy(a, shard, twin[1], 3 * nz + (z - s) * 2 + y).start()

        def from_right():
            shard = idx(z + s, y, c)
            got(a, shard)
            when(left[0], lambda: gcopy(a, shard, left[1], nz + z + s).start())
            cross(a, s, z + s)
            gcopy(a, shard, twin[1], 3 * nz + (z + s) * 2 + y).start()

        if s == 0:
            from_left()
        elif s < nz:
            pl.when(z - s >= 0)(from_left)
            pl.when(z + s < nz)(from_right)

    def y_step(s, a):
        def one(zz):
            shard = idx(zz, 1 - y, c)
            got(a, shard)
            gcopy(a, shard, twin[1], 3 * nz + zz * 2 + 1 - y).start()

        if s == 0:
            one(z)
            if GATHER_BYPASS[a]:
                gcopy(a, idx(z, 1 - y, c), partner, 5 * nz).start()
        elif s < nz:
            pl.when(z - s >= 0)(lambda: one(z - s))
            pl.when(z + s < nz)(lambda: one(z + s))

    def slot(k):
        m = jnp.minimum(z, nz - 1 - z)
        close = z - (k + 1) // 2 if k % 2 else z + k // 2
        far = jnp.where(2 * z < nz - 1, z + (k - m), z - (k - m))
        return jnp.where(k <= 2 * m, close, far)

    def to_twin(m, zz, yy):
        k = zz * 2 + yy
        return remote(
            parts[m].at[at(idx(zz, yy, 1 - c)), :], rd.at[m, k], dss.at[m, k], drs.at[m, k], twin[1]
        )

    def to_across(m, zz):
        return remote(ys.at[m, zz], ry.at[m, zz], yss.at[m, zz], yrs.at[m, zz], across[1])

    def to_right(m, zz):
        return remote(
            zs.at[m, zz], rz.at[m, zz + 1], zss.at[m, zz], zrs.at[m, zz + 1], right[1]
        )

    def to_left(m, zz):
        return remote(zs.at[m, zz], rz.at[m, zz], zss.at[m, zz], zrs.at[m, zz], left[1])

    def to_partner(m):
        return remote(ys.at[m, pz], rp.at[m], pss.at[m], prs.at[m], partner)

    def y_part(m, k):
        zz = slot(k)
        to_twin(m, zz, 1 - y).wait_recv()
        part = wide(parts[m][at(idx(zz, 1 - y, c)), :]) + wide(rd[m, zz * 2 + 1 - y])
        if k == 0 and SCATTER_BYPASS[m]:
            to_partner(m).wait_recv()
            part = part + wide(rp[m])
        ys[m, zz] = part.astype(BF)
        if k == 0 or not SCATTER_BYPASS[m]:
            to_across(m, zz).start()
        else:
            pl.when(zz != pz)(lambda: to_across(m, zz).start())
            pl.when(zz == pz)(lambda: to_partner(m).start())

    def own(m, zz):
        return wide(parts[m][at(idx(zz, y, c)), :]) + wide(rd[m, zz * 2 + y])

    def held(m, zz):
        to_across(m, zz).wait_recv()
        return own(m, zz) + wide(ry[m, zz])

    def z_part(m, k):
        zz = slot(k)
        to_twin(m, zz, y).wait_recv()
        if SCATTER_BYPASS[m]:

            @pl.when(zz != pz)
            def _():
                zs[m, zz] = held(m, zz).astype(BF)

            @pl.when(zz == pz)
            def _():
                zs[m, zz] = own(m, zz).astype(BF)

        else:
            zs[m, zz] = held(m, zz).astype(BF)

        @pl.when(zz > z)
        def _():
            @pl.when(z > 0)
            def _():
                to_right(m, zz).wait_recv()
                zs[m, zz] = (wide(zs[m, zz]) + wide(rz[m, zz + 1])).astype(BF)

            to_right(m, zz).start()

        @pl.when(zz < z)
        def _():
            @pl.when(z < nz - 1)
            def _():
                to_left(m, zz).wait_recv()
                zs[m, zz] = (wide(zs[m, zz]) + wide(rz[m, zz])).astype(BF)

            to_left(m, zz).start()

    def finish(m):
        to_twin(m, z, y).wait_recv()
        zs[m, z] = held(m, z).astype(BF)

        @pl.when(z > 0)
        def _():
            to_right(m, z).wait_recv()
            zs[m, z] = (wide(zs[m, z]) + wide(rz[m, z + 1])).astype(BF)

        @pl.when(z < nz - 1)
        def _():
            to_left(m, z).wait_recv()
            zs[m, z] = (wide(zs[m, z]) + wide(rz[m, z])).astype(BF)

        outs[m][...] = zs[m, z]

    def cols(q):
        return pl.ds(q * f, f)

    def prepare(q):
        loads[q].wait()
        fi = fin[q // 2, q % 2]
        fo = fout[q // 2, q % 2]
        ih = fi.astype(BF)
        il = (fi - wide(ih)).astype(BF)
        oh = fo.astype(BF)
        ol = (fo - wide(oh)).astype(BF)
        lhs = jnp.concatenate([ih, ih, il, il], axis=0)
        rhs = jnp.concatenate([oh, ol, oh, ol], axis=0)
        tile = 256
        total = jnp.zeros((8, f), F32)
        for t in range(width // tile):
            low = lax.dot_general(
                lhs[:, t * tile : (t + 1) * tile],
                rhs,
                (((0,), (0,)), ((), ())),
                preferred_element_type=F32,
            )
            part = wide(wv[q, pl.ds(t * tile, tile), :]) + ADAPTER_SCALE * low
            cm[pl.ds(t * tile, tile), cols(q)] = part.astype(BF)
            cmt[cols(q), pl.ds(t * tile, tile)] = part.astype(BF).T
            total = total + jnp.sum((part * part).reshape(tile // 8, 8, f), axis=0)
        total = jnp.sum(total, axis=0, keepdims=True) + NORM_EPS
        norm[q] = total
        scl[q] = gains[q // 2, q % 2 : q % 2 + 1] / jnp.sqrt(total)
        act[q] = jnp.zeros((8, f), F32)

    def turn_down():
        load_down.wait()
        for j in range(nj):
            for t in range(width // 256):
                wdt[pl.ds(t * 256, 256), pl.ds(j * f, f)] = wd[j, :, pl.ds(t * 256, 256)].T

    start = lax.axis_index("expert") * nj
    tile = 32
    lane = lax.broadcasted_iota(jnp.int32, (tile, 2 * half), 1)

    def gate_of(r, j):
        g = wide(xg[r, pl.ds(width, 2 * half)])
        mine = (lane == start + j) | (lane == start + j + half)
        return jnp.sum(jnp.where(mine, g, 0.0), axis=1, keepdims=True)

    def rise(k):
        zz = slot(k)
        base = zz * slab
        r = pl.ds(pl.multiple_of(base, slab), slab)
        for yy in range(2):
            got(0, idx(zz, yy, 1 - c))
        for j in range(nj):
            n = pl.ds(j * 2 * f, 2 * f)
            pr[r, n] = dot(xg[r, pl.ds(0, width)], cm[:, n])

        def gating(i, _):
            t = pl.ds(pl.multiple_of(base + i * tile, tile), tile)
            for j in range(nj):
                pre = pr[t, cols(2 * j)] * scl[2 * j]
                up = pr[t, cols(2 * j + 1)] * scl[2 * j + 1]
                hid[t, cols(j)] = (pre * jax.nn.sigmoid(pre) * up * gate_of(t, j)).astype(BF)
            return 0

        lax.fori_loop(0, slab // tile, gating, 0)

    def fall(k):
        zz = slot(k)
        r = pl.ds(pl.multiple_of(zz * slab, slab), slab)
        for t in range(width // 512):
            n = pl.ds(t * 512, 512)
            acc = dot(hid[r, cols(0)], wd[0, :, n])
            for j in range(1, nj):
                acc = acc + dot(hid[r, cols(j)], wd[j, :, n])
            pa[r, n] = acc.astype(BF)
        for yy in range(2):
            to_twin(0, zz, yy).start()

    def bend(k):
        zz = slot(k)
        base = zz * slab
        r = pl.ds(pl.multiple_of(base, slab), slab)
        for yy in range(2):
            got(1, idx(zz, yy, 1 - c))
        gh[...] = dot(cg[r, :], wdt[...])

        def gating(i, _):
            t = pl.ds(pl.multiple_of(base + i * tile, tile), tile)
            here = pl.ds(pl.multiple_of(i * tile, tile), tile)
            for j in range(nj):
                raw0 = pr[t, cols(2 * j)]
                raw1 = pr[t, cols(2 * j + 1)]
                s0 = scl[2 * j]
                s1 = scl[2 * j + 1]
                pre = raw0 * s0
                up = raw1 * s1
                s = jax.nn.sigmoid(pre)
                gr = gh[here, cols(j)] * gate_of(t, j)
                g0 = (gr * up * s * (1.0 + pre * (1.0 - s)) * s0).astype(BF)
                g1 = (gr * pre * s * s1).astype(BF)
                gp[t, cols(2 * j)] = g0
                gp[t, cols(2 * j + 1)] = g1
                for q, g, raw in ((2 * j, g0, raw0), (2 * j + 1, g1, raw1)):
                    term = wide(g) * raw
                    act[q] += jnp.sum(term.reshape(tile // 8, 8, f), axis=0)
            return 0

        lax.fori_loop(0, slab // tile, gating, 0)

    def back(k):
        zz = slot(k)
        r = pl.ds(pl.multiple_of(zz * slab, slab), slab)
        for t in range(width // 512):
            n = pl.ds(t * 512, 512)
            acc = dot(gp[r, pl.ds(0, 2 * f)], cmt[pl.ds(0, 2 * f), n])
            for j in range(1, nj):
                k2 = pl.ds(j * 2 * f, 2 * f)
                acc = acc + dot(gp[r, k2], cmt[k2, n])
            pb[r, n] = acc.astype(BF)
        for yy in range(2):
            to_twin(1, zz, yy).start()

    group = [pl.ds(q * rank, rank) for q in range(npair)]

    def low_in():
        ih = jnp.concatenate([fin[q // 2, q % 2] for q in range(npair)], axis=0).astype(BF)
        lowt[...] = dot_nt(ih, xg[:, pl.ds(0, width)])

    def low_out():
        for q in range(npair):
            tt[group[q], :] = dot_nt(fout[q // 2, q % 2].astype(BF), gp[:, cols(q)])
        inp[...] = dot(tt[...].astype(BF), xg[:, pl.ds(0, width)])

    def total_act(q):
        return jnp.sum(act[q], axis=0, keepdims=True)

    def in_part():
        for q in range(npair):
            curved = fout[q // 2, q % 2] * (total_act(q) / norm[q])
            low = dot(curved.astype(BF), cmt[cols(q), :])
            inp[group[q], :] = ADAPTER_SCALE * (inp[group[q], :] - low)
        swap_inp.start()

    def out_part(q):
        j, p = q // 2, q % 2
        total = total_act(q)
        first = dot(lowt[group[q], :].astype(BF), gp[:, cols(q)])
        second = dot(fin[j, p].astype(BF), cm[:, cols(q)]) * (total / norm[q])
        moved = MOMENTUM * out_mom[j, p] + ADAPTER_SCALE * (first - second)
        new_out_mom[j, p] = moved
        new_out[j, p] = fout[j, p] - LEARN_RATE * moved
        one = pl.ds(p, 1)
        bent = MOMENTUM * gain_mom[j, one, :] + total / gains[j, one, :]
        new_gain_mom[j, one, :] = bent
        new_gain[j, one, :] = gains[j, one, :] - LEARN_RATE * bent

    def in_finish():
        swap_mom.wait()
        swap_inp.wait()
        share = mom.shape[1]
        for own in range(2):
            k = pl.ds(pl.multiple_of((c if own else 1 - c) * share, share), share)
            old = mom[...] if own else rmom[...]
            moved = MOMENTUM * old + (inp[:, k] + rin[:, k])
            if own:
                new_mom[...] = moved
            for q in range(npair):
                new_in[q // 2, q % 2, :, k] = (
                    fin[q // 2, q % 2, :, k]
                    - LEARN_RATE * moved[q * rank : (q + 1) * rank]
                )

    swap_mom = remote(mom, rmom, ess.at[0], ers.at[0], twin[1])
    swap_inp = remote(inp, rin, ess.at[1], ers.at[1], twin[1])

    heard()
    extra = [low_in, low_out, in_part] + [functools.partial(out_part, q) for q in range(npair)]

    def filler():
        if extra:
            extra.pop(0)()

    turns = {
        "z": z_step,
        "y": y_step,
        "p": prepare,
        "t": turn_down,
        "m": lambda: swap_mom.start(),
        "U": rise,
        "D": fall,
        "V": bend,
        "W": back,
        "Y": y_part,
        "Z": z_part,
        "E": finish,
        "x": filler,
    }
    for turn in PLAN:
        turns[turn[0]](*turn[1:])
    while extra:
        filler()
    in_finish()
    for a in range(2):
        for zz in range(nz):
            pl.when(jnp.logical_and(z >= zz, z < nz - 1))(
                lambda: gcopy(a, idx(zz, y, c), right[1], zz).wait_send()
            )
            pl.when(jnp.logical_and(z <= zz, z > 0))(
                lambda: gcopy(a, idx(zz, y, c), left[1], nz + zz).wait_send()
            )
            crossed = gcopy(a, idx(zz, y, c), across[1], 2 * nz + zz)
            if GATHER_BYPASS[a]:
                pl.when(pz != zz)(lambda: crossed.wait_send())
            else:
                crossed.wait_send()
            for yy in range(2):
                gcopy(a, idx(zz, yy, c), twin[1], 3 * nz + zz * 2 + yy).wait_send()
        if GATHER_BYPASS[a]:
            gcopy(a, idx(z, 1 - y, c), partner, 5 * nz).wait_send()
    for m in range(2):
        for zz in range(nz):
            for yy in range(2):
                to_twin(m, zz, yy).wait_send()
            if SCATTER_BYPASS[m]:
                pl.when(pz != zz)(lambda: to_across(m, zz).wait_send())
            else:
                to_across(m, zz).wait_send()
            pl.when(z < zz)(lambda: to_right(m, zz).wait_send())
            pl.when(z > zz)(lambda: to_left(m, zz).wait_send())
        if SCATTER_BYPASS[m]:
            to_partner(m).wait_send()


def place_kernel(*refs):
    n = len(refs) // 2
    for k in range(n):
        refs[n + k][...] = refs[k][...]


VM = pl.BlockSpec(memory_space=pltpu.VMEM)
HBM = pl.BlockSpec(memory_space=pl.ANY)
DMA = pltpu.SemaphoreType.DMA


def gather(nz, tok, cot, ids, gates, w, fin, fout, gains, lanes):
    n = nz * 4
    rows, width = tok.shape
    j, p, d, f = w.shape
    return pl.pallas_call(
        functools.partial(gather_kernel, nz),
        out_shape=(
            jax.ShapeDtypeStruct((n, rows, width), BF),
            jax.ShapeDtypeStruct((n, rows, width), BF),
            jax.ShapeDtypeStruct((n, rows, lanes), F32),
            jax.ShapeDtypeStruct(w.shape, BF),
            jax.ShapeDtypeStruct((j, p, 1, f), F32),
        ),
        in_specs=[VM] * 8,
        out_specs=[VM] * 5,
        scratch_shapes=[pltpu.VMEM((d, f), F32), DMA((3, 5 * nz)), DMA((3, n))],
        compiler_params=pltpu.CompilerParams(
            collective_id=0, has_side_effects=True, vmem_limit_bytes=56 << 20
        ),
    )(tok, cot, ids, gates, w, fin, fout, gains)


def scatter(nz, pa, pb):
    n, rows, width = pa.shape
    row = jax.ShapeDtypeStruct((rows, width), BF)
    return pl.pallas_call(
        functools.partial(scatter_kernel, nz),
        out_shape=(row, row),
        in_specs=[VM] * 2,
        out_specs=[VM] * 2,
        scratch_shapes=[
            pltpu.VMEM((2, nz * 2, rows, width), BF),
            pltpu.VMEM((2, nz, rows, width), BF),
            pltpu.VMEM((2, nz, rows, width), BF),
            pltpu.VMEM((2, nz, rows, width), BF),
            pltpu.VMEM((2, nz + 1, rows, width), BF),
            DMA((2, nz * 2)),
            DMA((2, nz * 2)),
            DMA((2, nz)),
            DMA((2, nz)),
            DMA((2, nz)),
            DMA((2, nz + 1)),
        ],
        compiler_params=pltpu.CompilerParams(
            collective_id=1, has_side_effects=True, vmem_limit_bytes=56 << 20
        ),
    )(pa, pb)


def fused(nz, tok, cot, ids, gates, w, wd, fin, fout, gains, mom, out_mom, gain_mom):
    rows, width = tok.shape
    n = 4 * nz
    n_tok = n * rows
    nj, _, rank, f = fout.shape
    q = 2 * nj
    VMEM = pltpu.VMEM
    shape = jax.ShapeDtypeStruct
    row = shape((rows, width), BF)
    results = (
        row,
        row,
        shape(fin.shape, F32),
        shape(mom.shape, F32),
        shape(fout.shape, F32),
        shape(fout.shape, F32),
        shape(gains.shape, F32),
        shape(gains.shape, F32),
    )
    made = pl.pallas_call(
        functools.partial(fused_kernel, nz),
        out_shape=results,
        in_specs=[VM] * 4 + [HBM] * 2 + [VM] * 6,
        out_specs=[VM] * 8,
        scratch_shapes=[
            VMEM((n_tok, width + 128), BF),
            VMEM((n_tok, width), BF),
            VMEM((q, width, f), BF),
            VMEM((nj, f, width), BF),
            VMEM((width, nj * f), BF),
            VMEM((width, q * f), BF),
            VMEM((q * f, width), BF),
            VMEM((n_tok, q * f), F32),
            VMEM((4 * rows, nj * f), F32),
            VMEM((n_tok, nj * f), BF),
            VMEM((n_tok, q * f), BF),
            VMEM((q, 1, f), F32),
            VMEM((q, 1, f), F32),
            VMEM((q, 8, f), F32),
            VMEM((q * rank, width), F32),
            VMEM((q * rank, width), F32),
            VMEM(mom.shape, F32),
            VMEM((q * rank, n_tok), F32),
            VMEM((q * rank, n_tok), F32),
            VMEM((n_tok, width), BF),
            VMEM((n_tok, width), BF),
            VMEM((2, nz * 2, rows, width), BF),
            VMEM((2, nz, rows, width), BF),
            VMEM((2, nz, rows, width), BF),
            VMEM((2, nz, rows, width), BF),
            VMEM((2, nz + 1, rows, width), BF),
            DMA((q + 1,)),
            DMA((2, 5 * nz + 1)),
            DMA((2, n)),
            DMA((2, nz * 2)),
            DMA((2, nz * 2)),
            DMA((2, nz)),
            DMA((2, nz)),
            DMA((2, nz)),
            DMA((2, nz + 1)),
            DMA((2,)),
            DMA((2,)),
            DMA((2,)),
            DMA((2,)),
            VMEM((2, rows, width), BF),
        ],
        compiler_params=pltpu.CompilerParams(
            collective_id=2, has_side_effects=True, vmem_limit_bytes=58 << 20
        ),
    )(tok, cot, ids, gates, w, wd, fin, fout, gains, mom, out_mom, gain_mom)
    return pl.pallas_call(
        place_kernel,
        out_shape=results,
        in_specs=[VM] * 8,
        out_specs=[VM] * 8,
    )(*made)


def mm(spec, a, b):
    return jnp.einsum(spec, a, b, preferred_element_type=F32)


def update(
    new_mom_all, out_grad, gain_grad, input_factor, output_factor, gains,
    in_moment, out_moment, gain_moment,
):
    new_in = input_factor - LEARN_RATE * new_mom_all
    share = in_moment.shape[3]
    new_in_moment = lax.dynamic_slice_in_dim(new_mom_all, lax.axis_index("dp") * share, share, 3)
    new_out_moment = MOMENTUM * out_moment + out_grad
    new_out = output_factor - LEARN_RATE * new_out_moment
    new_gain_moment = MOMENTUM * gain_moment + gain_grad
    new_gains = gains - LEARN_RATE * new_gain_moment
    return new_in, new_in_moment, new_out, new_out_moment, new_gains, new_gain_moment


def body(
    tokens,
    route_ids,
    route_slots,
    route_gates,
    out_cotangent,
    gate_up_weight,
    w_down,
    input_factor,
    output_factor,
    gains,
    in_moment,
    out_moment,
    gain_moment,
):
    n_expert = lax.axis_size("expert")
    experts_here = w_down.shape[0]
    experts_all = experts_here * n_expert
    tok_here, width = tokens.shape
    nz = n_expert // 2
    lanes = -(-experts_all // 128) * 128
    n_all = 4 * nz * tok_here
    if n_all <= 1024 and experts_all <= 64 and nz == PLAN_NZ and experts_here == 2:
        share = in_moment.shape[3]
        mixed, token_grad, new_in, new_mom, *rest = fused(
            nz, tokens, out_cotangent, route_ids.T, route_gates.T, gate_up_weight, w_down,
            input_factor, output_factor, gains, in_moment.reshape(-1, share), out_moment,
            gain_moment,
        )
        return (mixed, token_grad, new_in, new_mom.reshape(in_moment.shape), *rest)
    x, c, g, merged, norm2 = gather(
        nz, tokens, out_cotangent, route_ids, route_gates, gate_up_weight,
        input_factor, output_factor, gains, lanes,
    )
    x = x.reshape(n_all, width)
    c = c.reshape(n_all, width)
    moment_all = lax.all_gather(in_moment, "dp", axis=3, tiled=True)
    norm2 = norm2[:, :, 0]
    col_norm = jnp.sqrt(norm2)
    col_scale = gains / col_norm
    moment_all = lax.all_gather(in_moment, "dp", axis=3, tiled=True)

    i_hi = input_factor.astype(BF)
    start = lax.axis_index("expert") * experts_here
    gate = lax.dynamic_slice_in_dim(g.reshape(n_all, lanes), start, experts_here, 1)
    gate = gate.T[:, :, None]

    projected = mm("td,jpdf->jptf", x, merged)
    gate_pre = projected[:, 0]
    up_pre = projected[:, 1]
    s = jax.nn.sigmoid(gate_pre)
    hidden = (gate_pre * s * up_pre * gate).astype(BF)
    grad_hidden = mm("td,jfd->jtf", c, w_down) * gate
    grad_gate = (grad_hidden * up_pre * s * (1.0 + gate_pre * (1.0 - s))).astype(BF)
    grad_up = (grad_hidden * gate_pre * s).astype(BF)
    grad_pair = jnp.stack([grad_gate, grad_up], axis=1)
    part_mixed = mm("jtf,jfd->td", hidden, w_down).astype(BF)
    part_grad = mm("jptf,jpdf->td", grad_pair, merged).astype(BF)
    split = (4 * nz, tok_here, width)
    mixed, token_grad = scatter(nz, part_mixed.reshape(split), part_grad.reshape(split))

    act_sum = jnp.sum(grad_pair.astype(F32) * projected, axis=2)
    gain_grad = act_sum / gains
    curvature = act_sum / norm2
    scaled_out = output_factor * col_scale[:, :, None, :]
    tilted = output_factor * (curvature / col_scale)[:, :, None, :]
    t_rows = mm("jptf,jprf->jptr", grad_pair, scaled_out.astype(BF))
    in_part = ADAPTER_SCALE * (
        mm("jptr,td->jprd", t_rows.astype(BF), x)
        - mm("jprf,jpdf->jprd", tilted.astype(BF), merged)
    )
    low_rows = mm("td,jprd->jptr", x, i_hi)
    out_grad = ADAPTER_SCALE * (
        mm("jptr,jptf->jprf", low_rows.astype(BF), grad_pair) * col_scale[:, :, None, :]
        - mm("jprd,jpdf->jprf", i_hi, merged) * (curvature / col_scale)[:, :, None, :]
    )
    n_dp = lax.axis_size("dp")
    mine = in_part
    pieces = lax.all_gather(mine, "dp", axis=0)
    in_grad = pieces[0]
    for k in range(1, n_dp):
        in_grad = in_grad + pieces[k]
    new_mom_all = MOMENTUM * moment_all + in_grad
    return (mixed, token_grad) + update(
        new_mom_all, out_grad, gain_grad, input_factor, output_factor, gains,
        in_moment, out_moment, gain_moment,
    )


def solution(mesh):
    return jax.shard_map(
        body,
        mesh=mesh,
        in_specs=(
            P(("groups", "expert", "dp"), None),
            P(("groups", "expert", "dp"), None),
            P(("groups", "expert", "dp"), None),
            P(("groups", "expert", "dp"), None),
            P(("groups", "expert", "dp"), None),
            P("expert", None, None, "dp"),
            P("expert", "dp", None),
            P("expert", None, None, None),
            P("expert", None, None, "dp"),
            P("expert", None, "dp"),
            P("expert", None, None, "dp"),
            P("expert", None, None, "dp"),
            P("expert", None, "dp"),
        ),
        out_specs=(
            P(("groups", "expert", "dp"), None),
            P(("groups", "expert", "dp"), None),
            P(("groups", "expert"), None, None, None),
            P(("groups", "expert"), None, None, "dp"),
            P(("groups", "expert"), None, None, "dp"),
            P(("groups", "expert"), None, None, "dp"),
            P(("groups", "expert"), None, "dp"),
            P(("groups", "expert"), None, "dp"),
        ),
        check_vma=False,
    )
```

```python
import functools

import jax
import jax.numpy as jnp
from jax import lax
from jax.experimental import pallas as pl
from jax.experimental.pallas import tpu as pltpu
from jax.sharding import PartitionSpec as P

ADAPTER_SCALE = 2.0
MOMENTUM = 0.9
LEARN_RATE = 0.05
NORM_EPS = 1e-06
BF = jnp.bfloat16
F32 = jnp.float32


MESH = pl.DeviceIdType.MESH


def place():
    e = lax.axis_index("expert")
    return lax.div(e, 2), lax.rem(e, 2), lax.axis_index("dp")


def near(z, y, c, nz):
    return (
        (z < nz - 1, {"expert": (z + 1) * 2 + y}),
        (z > 0, {"expert": (z - 1) * 2 + y}),
        (None, {"expert": z * 2 + 1 - y}),
        (None, {"dp": 1 - c}),
    )


def when(cond, fn):
    if cond is None:
        fn()
    else:
        pl.when(cond)(fn)


def hail(z, y, c, nz):
    barrier = pltpu.get_barrier_semaphore()
    for cond, dev in near(z, y, c, nz):
        when(
            cond,
            lambda dev=dev: pl.semaphore_signal(barrier, 1, device_id=dev, device_id_type=MESH),
        )
    inner = jnp.logical_and(z > 0, z < nz - 1)
    return lambda: pl.semaphore_wait(barrier, 3 + inner.astype(jnp.int32))


def greet(z, y, c, nz):
    hail(z, y, c, nz)()


def gather_kernel(
    nz, tok, cot, ids, gates, w, fin, fout, gains, xo, co, go, merged, norm, wide, ssem, rsem
):
    z, y, c = place()
    right, left, across, twin = near(z, y, c, nz)
    outs = (xo, co, go)

    def idx(zz, yy, cc):
        return (zz * 2 + yy) * 2 + cc

    def copy(a, shard, dev, slot):
        return pltpu.make_async_remote_copy(
            src_ref=outs[a].at[shard],
            dst_ref=outs[a].at[shard],
            send_sem=ssem.at[a, slot],
            recv_sem=rsem.at[a, shard],
            device_id=dev,
            device_id_type=MESH,
        )

    def send(shard, dev, slot):
        for a in range(3):
            copy(a, shard, dev, slot).start()

    def got(shard):
        for a in range(3):
            copy(a, shard, twin[1], 0).wait_recv()

    def sent(shard, dev, slot):
        for a in range(3):
            copy(a, shard, dev, slot).wait_send()

    me = idx(z, y, c)
    xo[me] = tok[...]
    co[me] = cot[...]
    rows = tok.shape[0]
    lanes = go.shape[2]
    col = lax.broadcasted_iota(jnp.int32, (rows, lanes), 1)
    dense = jnp.zeros((rows, lanes), F32)
    for k in range(ids.shape[1]):
        dense = dense + jnp.where(col == ids[:, k : k + 1], gates[:, k : k + 1], 0.0)
    go[me] = dense
    greet(z, y, c, nz)

    prep = [(j, p) for j in range(w.shape[0]) for p in range(w.shape[1])]

    def prepare():
        if not prep:
            return
        j, p = prep.pop(0)
        fi = fin[j, p]
        fo = fout[j, p]
        ih = fi.astype(BF)
        il = (fi - ih.astype(F32)).astype(BF)
        oh = fo.astype(BF)
        ol = (fo - oh.astype(F32)).astype(BF)
        lhs = jnp.concatenate([ih, ih, il, il], axis=0)
        rhs = jnp.concatenate([oh, ol, oh, ol], axis=0)
        width = w.shape[2]
        tile = 256
        total = jnp.zeros((1, w.shape[3]), F32)
        for t in range(width // tile):
            low = lax.dot_general(
                lhs[:, t * tile : (t + 1) * tile],
                rhs,
                (((0,), (0,)), ((), ())),
                preferred_element_type=F32,
            )
            part = w[j, p, pl.ds(t * tile, tile), :].astype(F32) + ADAPTER_SCALE * low
            wide[pl.ds(t * tile, tile), :] = part
            total = total + jnp.sum(part * part, axis=0, keepdims=True)
        total = total + NORM_EPS
        norm[j, p] = total
        scale = gains[j, p : p + 1] / jnp.sqrt(total)
        for t in range(width // tile):
            merged[j, p, pl.ds(t * tile, tile), :] = (
                wide[pl.ds(t * tile, tile), :] * scale
            ).astype(BF)

    def step_z(s):
        def from_left():
            shard = idx(z - s, y, c)
            if s:
                got(shard)
            when(right[0], lambda: send(shard, right[1], z - s))
            if not s:
                when(left[0], lambda: send(shard, left[1], nz + z))
            send(shard, across[1], 2 * nz + z - s)
            send(shard, twin[1], 3 * nz + (z - s) * 2 + y)

        def from_right():
            shard = idx(z + s, y, c)
            got(shard)
            when(left[0], lambda: send(shard, left[1], nz + z + s))
            send(shard, across[1], 2 * nz + z + s)
            send(shard, twin[1], 3 * nz + (z + s) * 2 + y)

        if s == 0:
            from_left()
        else:
            pl.when(z - s >= 0)(from_left)
            pl.when(z + s < nz)(from_right)

    def step_y(s):
        def one(zz):
            shard = idx(zz, 1 - y, c)
            got(shard)
            send(shard, twin[1], 3 * nz + zz * 2 + 1 - y)

        if s == 0:
            one(z)
        else:
            pl.when(z - s >= 0)(lambda: one(z - s))
            pl.when(z + s < nz)(lambda: one(z + s))

    step_z(0)
    prepare()
    for s in range(1, nz):
        step_z(s)
        step_y(s - 1)
        prepare()
    step_y(nz - 1)
    while prep:
        prepare()
    for zz in range(nz):
        for yy in range(2):
            got(idx(zz, yy, 1 - c))
    for zz in range(nz):
        here = z >= zz
        pl.when(jnp.logical_and(here, z < nz - 1))(
            lambda: sent(idx(zz, y, c), right[1], zz)
        )
        there = z <= zz
        pl.when(jnp.logical_and(there, z > 0))(
            lambda: sent(idx(zz, y, c), left[1], nz + zz)
        )
        sent(idx(zz, y, c), across[1], 2 * nz + zz)
        for yy in range(2):
            sent(idx(zz, yy, c), twin[1], 3 * nz + zz * 2 + yy)


def scatter_kernel(nz, pa, pb, oa, ob, rd, ys, ry, zs, rz, dss, drs, yss, yrs, zss, zrs):
    z, y, c = place()
    right, left, across, twin = near(z, y, c, nz)
    parts = (pa, pb)
    outs = (oa, ob)

    def idx(zz, yy, cc):
        return (zz * 2 + yy) * 2 + cc

    def remote(src, dst, a, b, dev):
        return pltpu.make_async_remote_copy(
            src_ref=src, dst_ref=dst, send_sem=a, recv_sem=b, device_id=dev, device_id_type=MESH
        )

    def to_twin(m, zz, yy):
        k = zz * 2 + yy
        return remote(
            parts[m].at[idx(zz, yy, 1 - c)], rd.at[m, k], dss.at[m, k], drs.at[m, k], twin[1]
        )

    def to_across(m, zz):
        return remote(ys.at[m, zz], ry.at[m, zz], yss.at[m, zz], yrs.at[m, zz], across[1])

    def to_right(m, zz):
        return remote(
            zs.at[m, zz], rz.at[m, zz + 1], zss.at[m, zz], zrs.at[m, zz + 1], right[1]
        )

    def to_left(m, zz):
        return remote(zs.at[m, zz], rz.at[m, zz], zss.at[m, zz], zrs.at[m, zz], left[1])

    def wide(v):
        return v.astype(F32)

    greet(z, y, c, nz)

    def each(s, fn):
        if s == 0:
            fn(z)
        else:
            pl.when(z + s < nz)(lambda: fn(z + s))
            pl.when(z - s >= 0)(lambda: fn(z - s))

    order = list(range(nz - 1, -1, -1))
    for m in range(2):
        for s in order:
            each(s, lambda zz: to_twin(m, zz, 1 - y).start())
        for s in order:
            each(s, lambda zz: to_twin(m, zz, y).start())

    def y_part(m, s):
        def one(zz):
            to_twin(m, zz, 1 - y).wait_recv()
            ys[m, zz] = (
                wide(parts[m][idx(zz, 1 - y, c)]) + wide(rd[m, zz * 2 + 1 - y])
            ).astype(BF)
            to_across(m, zz).start()

        each(s, one)

    def held(m, zz):
        to_twin(m, zz, y).wait_recv()
        to_across(m, zz).wait_recv()
        return wide(parts[m][idx(zz, y, c)]) + wide(rd[m, zz * 2 + y]) + wide(ry[m, zz])

    def z_part(m, s):
        def rightward():
            zz = z + s
            zs[m, zz] = held(m, zz).astype(BF)

            @pl.when(z > 0)
            def _():
                to_right(m, zz).wait_recv()
                zs[m, zz] = (wide(zs[m, zz]) + wide(rz[m, zz + 1])).astype(BF)

            to_right(m, zz).start()

        def leftward():
            zz = z - s
            zs[m, zz] = held(m, zz).astype(BF)

            @pl.when(z < nz - 1)
            def _():
                to_left(m, zz).wait_recv()
                zs[m, zz] = (wide(zs[m, zz]) + wide(rz[m, zz])).astype(BF)

            to_left(m, zz).start()

        pl.when(z + s < nz)(rightward)
        pl.when(z - s >= 0)(leftward)

    for m in range(2):
        for s in order:
            y_part(m, s)
    for m in range(2):
        for s in order[:-1]:
            z_part(m, s)
        zs[m, z] = held(m, z).astype(BF)

        @pl.when(z > 0)
        def _():
            to_right(m, z).wait_recv()
            zs[m, z] = (wide(zs[m, z]) + wide(rz[m, z + 1])).astype(BF)

        @pl.when(z < nz - 1)
        def _():
            to_left(m, z).wait_recv()
            zs[m, z] = (wide(zs[m, z]) + wide(rz[m, z])).astype(BF)

        outs[m][...] = zs[m, z]
    for m in range(2):
        for zz in range(nz):
            for yy in range(2):
                to_twin(m, zz, yy).wait_send()
            to_across(m, zz).wait_send()
            pl.when(z < zz)(lambda: to_right(m, zz).wait_send())
            pl.when(z > zz)(lambda: to_left(m, zz).wait_send())


GATHER_BYPASS = (False, False, True, True)
SCATTER_BYPASS = (True, True, False, False)
PLAN_NZ = 4
PLAN = (
    (1, "z", 0, 0), (1, "z", 0, 1), (0, "z", 0, 0), (0, "z", 0, 1), (2, "p", 0),
    (0, "z", 0, 2), (0, "z", 0, 3), (1, "z", 0, 2), (1, "z", 0, 3), (2, "t"), (2, "p", 1),
    (2, "p", 3), (1, "z", 1, 0), (1, "z", 1, 1), (2, "p", 2), (1, "z", 1, 2), (1, "z", 1, 3),
    (0, "y", 0, 0), (0, "y", 0, 1), (1, "z", 2, 0), (1, "z", 2, 1), (1, "y", 0, 0),
    (1, "y", 0, 1), (1, "y", 1, 0), (1, "y", 1, 1), (1, "z", 2, 2), (1, "z", 2, 3),
    (1, "z", 3, 0), (1, "z", 3, 1), (0, "z", 1, 0), (0, "z", 1, 1), (1, "y", 0, 2),
    (1, "y", 0, 3), (2, "U", 0), (0, "z", 5, 0), (0, "z", 5, 1), (0, "y", 1, 0),
    (0, "y", 1, 1), (0, "z", 2, 0), (0, "z", 2, 1), (0, "z", 1, 2), (0, "z", 1, 3),
    (2, "U", 1), (0, "z", 2, 2), (0, "z", 2, 3), (2, "D", 0), (0, "y", 2, 0), (0, "y", 2, 1),
    (1, "z", 3, 2), (1, "z", 3, 3), (0, "y", 0, 2), (0, "y", 0, 3), (1, "z", 4, 0),
    (1, "z", 4, 1), (1, "y", 1, 2), (1, "y", 1, 3), (1, "y", 2, 0), (1, "y", 2, 1),
    (0, "z", 4, 0), (0, "z", 4, 1), (0, "z", 3, 0), (0, "z", 3, 1), (2, "D", 1),
    (1, "z", 5, 0), (1, "z", 5, 1), (0, "z", 3, 2), (0, "z", 3, 3), (2, "U", 2),
    (0, "Y", 0, 1), (0, "Y", 1, 1), (0, "y", 3, 0), (0, "y", 3, 1), (1, "y", 3, 0),
    (1, "y", 3, 1), (2, "U", 3), (1, "y", 2, 2), (1, "y", 2, 3), (2, "D", 3), (1, "Y", 0, 3),
    (1, "Y", 1, 3), (0, "Y", 0, 3), (0, "Y", 1, 3), (0, "y", 1, 2), (0, "y", 1, 3),
    (2, "D", 2), (1, "y", 3, 2), (1, "y", 3, 3), (0, "y", 2, 2), (0, "y", 2, 3), (2, "V", 2),
    (0, "Y", 0, 2), (0, "Y", 1, 2), (2, "W", 2), (1, "Y", 0, 1), (1, "Y", 1, 1),
    (0, "Y", 2, 2), (0, "Y", 3, 2), (0, "y", 3, 2), (0, "y", 3, 3), (0, "Z", 0, 3),
    (0, "Z", 1, 3), (1, "Y", 0, 2), (1, "Y", 1, 2), (2, "V", 3), (2, "W", 3), (0, "Z", 0, 2),
    (0, "Z", 1, 2), (1, "Y", 2, 3), (1, "Y", 3, 3), (1, "Z", 0, 3), (1, "Z", 1, 3),
    (0, "Y", 2, 3), (0, "Y", 3, 3), (2, "x"), (2, "V", 1), (2, "W", 1), (1, "Y", 2, 2),
    (1, "Y", 3, 2), (0, "Z", 2, 3), (0, "Z", 3, 3), (1, "Z", 0, 2), (1, "Z", 1, 2),
    (1, "Z", 0, 1), (1, "Z", 1, 1), (0, "Z", 2, 2), (0, "Z", 3, 2), (1, "Y", 2, 1),
    (1, "Y", 3, 1), (0, "Y", 2, 1), (0, "Y", 3, 1), (2, "V", 0), (1, "Z", 2, 3),
    (1, "Z", 3, 3), (2, "x"), (0, "Y", 0, 0), (0, "Y", 1, 0), (1, "Y", 0, 0), (1, "Y", 1, 0),
    (2, "W", 0), (2, "x"), (1, "Y", 2, 0), (1, "Y", 3, 0), (0, "Z", 0, 1), (0, "Z", 1, 1),
    (1, "Z", 2, 2), (1, "Z", 3, 2), (0, "Y", 2, 0), (0, "Y", 3, 0), (1, "Z", 2, 1),
    (1, "Z", 3, 1), (0, "Z", 2, 1), (0, "Z", 3, 1), (2, "x"), (2, "x"), (2, "x"), (1, "E", 0),
    (1, "E", 1), (2, "m"), (2, "x"), (0, "E", 0), (0, "E", 1), (1, "E", 2), (1, "E", 3),
    (0, "E", 2), (0, "E", 3),
)


def fused_kernel(
    nz, tok, cot, ids, gates, w, wd_in, fin, fout, gains, mom, out_mom, gain_mom,
    mixed, token_grad, new_in, new_mom, new_out, new_out_mom, new_gain, new_gain_mom,
    xg, cg, wv, wd, wdt, cm, cmt, pr, gh, hid, gp, norm, scl, act, inp, rin, rmom, lowt, tt,
    pa, pb, rd, ys, ry, zs, rz,
    lsem, gss, grs, dss, drs, yss, yrs, zss, zrs, ess, ers, pss, prs, rp,
):
    z, y, c = place()
    right, left, across, twin = near(z, y, c, nz)
    pz = z + 1 - 2 * lax.rem(z, 2)
    partner = {"expert": pz * 2 + y}
    heard = hail(z, y, c, nz)
    parts = (pa, pb)
    outs = (mixed, token_grad)
    rows, width = tok.shape
    nj, _, rank, f = fout.shape
    npair = 2 * nj
    slab = 4 * rows

    def idx(zz, yy, cc):
        return (zz * 2 + yy) * 2 + cc

    def dot(u, v):
        return jnp.dot(u, v, preferred_element_type=F32)

    def dot_nt(u, v):
        return lax.dot_general(u, v, (((1,), (1,)), ((), ())), preferred_element_type=F32)

    def wide(v):
        return v.astype(F32)

    def at(shard):
        return pl.ds(pl.multiple_of(shard * rows, rows), rows)

    hr = rows // 2

    def at_half(shard, m):
        return pl.ds(pl.multiple_of(shard * rows + (m % 2) * hr, hr), hr)

    def remote(src, dst, a, b, dev):
        return pltpu.make_async_remote_copy(
            src_ref=src, dst_ref=dst, send_sem=a, recv_sem=b, device_id=dev, device_id_type=MESH
        )

    loads = [
        pltpu.make_async_copy(w.at[q // 2, q % 2], wv.at[q], lsem.at[q]) for q in range(npair)
    ]
    load_down = pltpu.make_async_copy(wd_in, wd, lsem.at[npair])
    for load in loads:
        load.start()
    load_down.start()

    me = idx(z, y, c)
    half = (xg.shape[1] - width) // 2
    row = lax.broadcasted_iota(jnp.int32, (half, rows), 0)
    dense = jnp.zeros((half, rows), F32)
    for k in range(ids.shape[0]):
        dense = dense + jnp.where(row == ids[k : k + 1, :], gates[k : k + 1, :], 0.0)
    high = dense.astype(BF)
    both = jnp.concatenate([high, (dense - wide(high)).astype(BF)], axis=0)
    eye = (
        lax.broadcasted_iota(jnp.int32, (rows, rows), 0)
        == lax.broadcasted_iota(jnp.int32, (rows, rows), 1)
    ).astype(BF)
    xg[at(me), pl.ds(0, width)] = tok[...]
    xg[at(me), pl.ds(width, 2 * half)] = dot_nt(eye, both).astype(BF)
    cg[at(me), :] = cot[...]

    held_rows = (xg, cg)

    def gcopy(a, shard, dev, s):
        ref = held_rows[a // 2].at[at_half(shard, a), :]
        return remote(ref, ref, gss.at[a, s], grs.at[a, shard], dev)

    def got(a, shard):
        gcopy(a, shard, twin[1], 0).wait_recv()

    def cross(a, s, zz):
        send = gcopy(a, idx(zz, y, c), across[1], 2 * nz + zz)
        if GATHER_BYPASS[a] and s == 1:
            pl.when(zz != pz)(lambda: send.start())
        else:
            send.start()

    def z_step(s, a):
        def from_left():
            shard = idx(z - s, y, c)
            if s:
                got(a, shard)
            when(right[0], lambda: gcopy(a, shard, right[1], z - s).start())
            if not s:
                when(left[0], lambda: gcopy(a, shard, left[1], nz + z).start())
            cross(a, s, z - s)
            gcopy(a, shard, twin[1], 3 * nz + (z - s) * 2 + y).start()

        def from_right():
            shard = idx(z + s, y, c)
            got(a, shard)
            when(left[0], lambda: gcopy(a, shard, left[1], nz + z + s).start())
            cross(a, s, z + s)
            gcopy(a, shard, twin[1], 3 * nz + (z + s) * 2 + y).start()

        if s == 0:
            from_left()
        elif s < nz:
            pl.when(z - s >= 0)(from_left)
            pl.when(z + s < nz)(from_right)

    def y_step(s, a):
        def one(zz):
            shard = idx(zz, 1 - y, c)
            got(a, shard)
            gcopy(a, shard, twin[1], 3 * nz + zz * 2 + 1 - y).start()

        if s == 0:
            one(z)
            if GATHER_BYPASS[a]:
                gcopy(a, idx(z, 1 - y, c), partner, 5 * nz).start()
        elif s < nz:
            pl.when(z - s >= 0)(lambda: one(z - s))
            pl.when(z + s < nz)(lambda: one(z + s))

    def slot(k):
        m = jnp.minimum(z, nz - 1 - z)
        close = z - (k + 1) // 2 if k % 2 else z + k // 2
        far = jnp.where(2 * z < nz - 1, z + (k - m), z - (k - m))
        return jnp.where(k <= 2 * m, close, far)

    def to_twin(m, zz, yy):
        k = zz * 2 + yy
        return remote(
            parts[m // 2].at[at_half(idx(zz, yy, 1 - c), m), :],
            rd.at[m, k],
            dss.at[m, k],
            drs.at[m, k],
            twin[1],
        )

    def to_across(m, zz):
        return remote(ys.at[m, zz], ry.at[m, zz], yss.at[m, zz], yrs.at[m, zz], across[1])

    def to_right(m, zz):
        return remote(
            zs.at[m, zz], rz.at[m, zz + 1], zss.at[m, zz], zrs.at[m, zz + 1], right[1]
        )

    def to_left(m, zz):
        return remote(zs.at[m, zz], rz.at[m, zz], zss.at[m, zz], zrs.at[m, zz], left[1])

    def to_partner(m):
        return remote(ys.at[m, pz], rp.at[m], pss.at[m], prs.at[m], partner)

    def y_part(m, k):
        zz = slot(k)
        to_twin(m, zz, 1 - y).wait_recv()
        part = wide(parts[m // 2][at_half(idx(zz, 1 - y, c), m), :]) + wide(
            rd[m, zz * 2 + 1 - y]
        )
        if k == 0 and SCATTER_BYPASS[m]:
            to_partner(m).wait_recv()
            part = part + wide(rp[m])
        ys[m, zz] = part.astype(BF)
        if k == 0 or not SCATTER_BYPASS[m]:
            to_across(m, zz).start()
        else:
            pl.when(zz != pz)(lambda: to_across(m, zz).start())
            pl.when(zz == pz)(lambda: to_partner(m).start())

    def own(m, zz):
        return wide(parts[m // 2][at_half(idx(zz, y, c), m), :]) + wide(rd[m, zz * 2 + y])

    def held(m, zz):
        to_across(m, zz).wait_recv()
        return own(m, zz) + wide(ry[m, zz])

    def z_part(m, k):
        zz = slot(k)
        to_twin(m, zz, y).wait_recv()
        if SCATTER_BYPASS[m]:

            @pl.when(zz != pz)
            def _():
                zs[m, zz] = held(m, zz).astype(BF)

            @pl.when(zz == pz)
            def _():
                zs[m, zz] = own(m, zz).astype(BF)

        else:
            zs[m, zz] = held(m, zz).astype(BF)

        @pl.when(zz > z)
        def _():
            @pl.when(z > 0)
            def _():
                to_right(m, zz).wait_recv()
                zs[m, zz] = (wide(zs[m, zz]) + wide(rz[m, zz + 1])).astype(BF)

            to_right(m, zz).start()

        @pl.when(zz < z)
        def _():
            @pl.when(z < nz - 1)
            def _():
                to_left(m, zz).wait_recv()
                zs[m, zz] = (wide(zs[m, zz]) + wide(rz[m, zz])).astype(BF)

            to_left(m, zz).start()

    def finish(m):
        to_twin(m, z, y).wait_recv()
        zs[m, z] = held(m, z).astype(BF)

        @pl.when(z > 0)
        def _():
            to_right(m, z).wait_recv()
            zs[m, z] = (wide(zs[m, z]) + wide(rz[m, z + 1])).astype(BF)

        @pl.when(z < nz - 1)
        def _():
            to_left(m, z).wait_recv()
            zs[m, z] = (wide(zs[m, z]) + wide(rz[m, z])).astype(BF)

        outs[m // 2][pl.ds((m % 2) * hr, hr), :] = zs[m, z]

    def cols(q):
        return pl.ds(q * f, f)

    def prepare(q):
        loads[q].wait()
        fi = fin[q // 2, q % 2]
        fo = fout[q // 2, q % 2]
        ih = fi.astype(BF)
        il = (fi - wide(ih)).astype(BF)
        oh = fo.astype(BF)
        ol = (fo - wide(oh)).astype(BF)
        lhs = jnp.concatenate([ih, ih, il, il], axis=0)
        rhs = jnp.concatenate([oh, ol, oh, ol], axis=0)
        tile = 256
        total = jnp.zeros((8, f), F32)
        for t in range(width // tile):
            low = lax.dot_general(
                lhs[:, t * tile : (t + 1) * tile],
                rhs,
                (((0,), (0,)), ((), ())),
                preferred_element_type=F32,
            )
            part = wide(wv[q, pl.ds(t * tile, tile), :]) + ADAPTER_SCALE * low
            cm[pl.ds(t * tile, tile), cols(q)] = part.astype(BF)
            cmt[cols(q), pl.ds(t * tile, tile)] = part.astype(BF).T
            total = total + jnp.sum((part * part).reshape(tile // 8, 8, f), axis=0)
        total = jnp.sum(total, axis=0, keepdims=True) + NORM_EPS
        norm[q] = total
        scl[q] = gains[q // 2, q % 2 : q % 2 + 1] / jnp.sqrt(total)
        act[q] = jnp.zeros((8, f), F32)

    def turn_down():
        load_down.wait()
        for j in range(nj):
            for t in range(width // 256):
                wdt[pl.ds(t * 256, 256), pl.ds(j * f, f)] = wd[j, :, pl.ds(t * 256, 256)].T

    start = lax.axis_index("expert") * nj
    tile = 32
    lane = lax.broadcasted_iota(jnp.int32, (tile, 2 * half), 1)

    def gate_of(r, j):
        g = wide(xg[r, pl.ds(width, 2 * half)])
        mine = (lane == start + j) | (lane == start + j + half)
        return jnp.sum(jnp.where(mine, g, 0.0), axis=1, keepdims=True)

    def rise(k):
        zz = slot(k)
        base = zz * slab
        r = pl.ds(pl.multiple_of(base, slab), slab)
        for yy in range(2):
            got(0, idx(zz, yy, 1 - c))
            got(1, idx(zz, yy, 1 - c))
        for j in range(nj):
            n = pl.ds(j * 2 * f, 2 * f)
            pr[r, n] = dot(xg[r, pl.ds(0, width)], cm[:, n])

        def gating(i, _):
            t = pl.ds(pl.multiple_of(base + i * tile, tile), tile)
            for j in range(nj):
                pre = pr[t, cols(2 * j)] * scl[2 * j]
                up = pr[t, cols(2 * j + 1)] * scl[2 * j + 1]
                hid[t, cols(j)] = (pre * jax.nn.sigmoid(pre) * up * gate_of(t, j)).astype(BF)
            return 0

        lax.fori_loop(0, slab // tile, gating, 0)

    def fall(k):
        zz = slot(k)
        r = pl.ds(pl.multiple_of(zz * slab, slab), slab)
        for t in range(width // 512):
            n = pl.ds(t * 512, 512)
            acc = dot(hid[r, cols(0)], wd[0, :, n])
            for j in range(1, nj):
                acc = acc + dot(hid[r, cols(j)], wd[j, :, n])
            pa[r, n] = acc.astype(BF)
        for yy in range(2):
            to_twin(0, zz, yy).start()
            to_twin(1, zz, yy).start()

    def bend(k):
        zz = slot(k)
        base = zz * slab
        r = pl.ds(pl.multiple_of(base, slab), slab)
        for yy in range(2):
            got(2, idx(zz, yy, 1 - c))
            got(3, idx(zz, yy, 1 - c))
        gh[...] = dot(cg[r, :], wdt[...])

        def gating(i, _):
            t = pl.ds(pl.multiple_of(base + i * tile, tile), tile)
            here = pl.ds(pl.multiple_of(i * tile, tile), tile)
            for j in range(nj):
                raw0 = pr[t, cols(2 * j)]
                raw1 = pr[t, cols(2 * j + 1)]
                s0 = scl[2 * j]
                s1 = scl[2 * j + 1]
                pre = raw0 * s0
                up = raw1 * s1
                s = jax.nn.sigmoid(pre)
                gr = gh[here, cols(j)] * gate_of(t, j)
                g0 = (gr * up * s * (1.0 + pre * (1.0 - s)) * s0).astype(BF)
                g1 = (gr * pre * s * s1).astype(BF)
                gp[t, cols(2 * j)] = g0
                gp[t, cols(2 * j + 1)] = g1
                for q, g, raw in ((2 * j, g0, raw0), (2 * j + 1, g1, raw1)):
                    term = wide(g) * raw
                    act[q] += jnp.sum(term.reshape(tile // 8, 8, f), axis=0)
            return 0

        lax.fori_loop(0, slab // tile, gating, 0)

    def back(k):
        zz = slot(k)
        r = pl.ds(pl.multiple_of(zz * slab, slab), slab)
        for t in range(width // 512):
            n = pl.ds(t * 512, 512)
            acc = dot(gp[r, pl.ds(0, 2 * f)], cmt[pl.ds(0, 2 * f), n])
            for j in range(1, nj):
                k2 = pl.ds(j * 2 * f, 2 * f)
                acc = acc + dot(gp[r, k2], cmt[k2, n])
            pb[r, n] = acc.astype(BF)
        for yy in range(2):
            to_twin(2, zz, yy).start()
            to_twin(3, zz, yy).start()

    group = [pl.ds(q * rank, rank) for q in range(npair)]

    def low_in():
        ih = jnp.concatenate([fin[q // 2, q % 2] for q in range(npair)], axis=0).astype(BF)
        lowt[...] = dot_nt(ih, xg[:, pl.ds(0, width)])

    def low_out():
        for q in range(npair):
            tt[group[q], :] = dot_nt(fout[q // 2, q % 2].astype(BF), gp[:, cols(q)])
        inp[...] = dot(tt[...].astype(BF), xg[:, pl.ds(0, width)])

    def total_act(q):
        return jnp.sum(act[q], axis=0, keepdims=True)

    def in_part():
        for q in range(npair):
            curved = fout[q // 2, q % 2] * (total_act(q) / norm[q])
            low = dot(curved.astype(BF), cmt[cols(q), :])
            inp[group[q], :] = ADAPTER_SCALE * (inp[group[q], :] - low)
        swap_inp.start()

    def out_part(q):
        j, p = q // 2, q % 2
        total = total_act(q)
        first = dot(lowt[group[q], :].astype(BF), gp[:, cols(q)])
        second = dot(fin[j, p].astype(BF), cm[:, cols(q)]) * (total / norm[q])
        moved = MOMENTUM * out_mom[j, p] + ADAPTER_SCALE * (first - second)
        new_out_mom[j, p] = moved
        new_out[j, p] = fout[j, p] - LEARN_RATE * moved
        one = pl.ds(p, 1)
        bent = MOMENTUM * gain_mom[j, one, :] + total / gains[j, one, :]
        new_gain_mom[j, one, :] = bent
        new_gain[j, one, :] = gains[j, one, :] - LEARN_RATE * bent

    def in_finish():
        swap_mom.wait()
        swap_inp.wait()
        share = mom.shape[1]
        for own in range(2):
            k = pl.ds(pl.multiple_of((c if own else 1 - c) * share, share), share)
            old = mom[...] if own else rmom[...]
            moved = MOMENTUM * old + (inp[:, k] + rin[:, k])
            if own:
                new_mom[...] = moved
            for q in range(npair):
                new_in[q // 2, q % 2, :, k] = (
                    fin[q // 2, q % 2, :, k]
                    - LEARN_RATE * moved[q * rank : (q + 1) * rank]
                )

    swap_mom = remote(mom, rmom, ess.at[0], ers.at[0], twin[1])
    swap_inp = remote(inp, rin, ess.at[1], ers.at[1], twin[1])

    heard()
    extra = [low_in, low_out, in_part] + [functools.partial(out_part, q) for q in range(npair)]

    def filler():
        if extra:
            extra.pop(0)()

    turns = {
        "z": z_step,
        "y": y_step,
        "p": prepare,
        "t": turn_down,
        "m": lambda: swap_mom.start(),
        "U": rise,
        "D": fall,
        "V": bend,
        "W": back,
        "Y": y_part,
        "Z": z_part,
        "E": finish,
        "x": filler,
    }
    edge = (z == 0) | (z == nz - 1)
    some = ([], [])

    def flush():
        def go(which):
            for name, *args in which:
                turns[name](*args)

        first, second = list(some[0]), list(some[1])
        while first and second and first[0] == second[0]:
            go([first.pop(0)])
            second.pop(0)
        if first:
            pl.when(edge)(functools.partial(go, first))
        if second:
            pl.when(jnp.logical_not(edge))(functools.partial(go, second))
        some[0].clear()
        some[1].clear()

    for tag, *turn in PLAN:
        if tag < 2:
            some[tag].append(tuple(turn))
        else:
            flush()
            turns[turn[0]](*turn[1:])
    flush()
    while extra:
        filler()
    in_finish()
    for a in range(4):
        for zz in range(nz):
            pl.when(jnp.logical_and(z >= zz, z < nz - 1))(
                lambda: gcopy(a, idx(zz, y, c), right[1], zz).wait_send()
            )
            pl.when(jnp.logical_and(z <= zz, z > 0))(
                lambda: gcopy(a, idx(zz, y, c), left[1], nz + zz).wait_send()
            )
            crossed = gcopy(a, idx(zz, y, c), across[1], 2 * nz + zz)
            if GATHER_BYPASS[a]:
                pl.when(pz != zz)(lambda: crossed.wait_send())
            else:
                crossed.wait_send()
            for yy in range(2):
                gcopy(a, idx(zz, yy, c), twin[1], 3 * nz + zz * 2 + yy).wait_send()
        if GATHER_BYPASS[a]:
            gcopy(a, idx(z, 1 - y, c), partner, 5 * nz).wait_send()
    for m in range(4):
        for zz in range(nz):
            for yy in range(2):
                to_twin(m, zz, yy).wait_send()
            if SCATTER_BYPASS[m]:
                pl.when(pz != zz)(lambda: to_across(m, zz).wait_send())
            else:
                to_across(m, zz).wait_send()
            pl.when(z < zz)(lambda: to_right(m, zz).wait_send())
            pl.when(z > zz)(lambda: to_left(m, zz).wait_send())
        if SCATTER_BYPASS[m]:
            to_partner(m).wait_send()


def place_kernel(*refs):
    n = len(refs) // 2
    for k in range(n):
        refs[n + k][...] = refs[k][...]


VM = pl.BlockSpec(memory_space=pltpu.VMEM)
HBM = pl.BlockSpec(memory_space=pl.ANY)
DMA = pltpu.SemaphoreType.DMA


def gather(nz, tok, cot, ids, gates, w, fin, fout, gains, lanes):
    n = nz * 4
    rows, width = tok.shape
    j, p, d, f = w.shape
    return pl.pallas_call(
        functools.partial(gather_kernel, nz),
        out_shape=(
            jax.ShapeDtypeStruct((n, rows, width), BF),
            jax.ShapeDtypeStruct((n, rows, width), BF),
            jax.ShapeDtypeStruct((n, rows, lanes), F32),
            jax.ShapeDtypeStruct(w.shape, BF),
            jax.ShapeDtypeStruct((j, p, 1, f), F32),
        ),
        in_specs=[VM] * 8,
        out_specs=[VM] * 5,
        scratch_shapes=[pltpu.VMEM((d, f), F32), DMA((3, 5 * nz)), DMA((3, n))],
        compiler_params=pltpu.CompilerParams(
            collective_id=0, has_side_effects=True, vmem_limit_bytes=56 << 20
        ),
    )(tok, cot, ids, gates, w, fin, fout, gains)


def scatter(nz, pa, pb):
    n, rows, width = pa.shape
    row = jax.ShapeDtypeStruct((rows, width), BF)
    return pl.pallas_call(
        functools.partial(scatter_kernel, nz),
        out_shape=(row, row),
        in_specs=[VM] * 2,
        out_specs=[VM] * 2,
        scratch_shapes=[
            pltpu.VMEM((2, nz * 2, rows, width), BF),
            pltpu.VMEM((2, nz, rows, width), BF),
            pltpu.VMEM((2, nz, rows, width), BF),
            pltpu.VMEM((2, nz, rows, width), BF),
            pltpu.VMEM((2, nz + 1, rows, width), BF),
            DMA((2, nz * 2)),
            DMA((2, nz * 2)),
            DMA((2, nz)),
            DMA((2, nz)),
            DMA((2, nz)),
            DMA((2, nz + 1)),
        ],
        compiler_params=pltpu.CompilerParams(
            collective_id=1, has_side_effects=True, vmem_limit_bytes=56 << 20
        ),
    )(pa, pb)


def fused(nz, tok, cot, ids, gates, w, wd, fin, fout, gains, mom, out_mom, gain_mom):
    rows, width = tok.shape
    n = 4 * nz
    n_tok = n * rows
    nj, _, rank, f = fout.shape
    q = 2 * nj
    VMEM = pltpu.VMEM
    shape = jax.ShapeDtypeStruct
    row = shape((rows, width), BF)
    results = (
        row,
        row,
        shape(fin.shape, F32),
        shape(mom.shape, F32),
        shape(fout.shape, F32),
        shape(fout.shape, F32),
        shape(gains.shape, F32),
        shape(gains.shape, F32),
    )
    made = pl.pallas_call(
        functools.partial(fused_kernel, nz),
        out_shape=results,
        in_specs=[VM] * 4 + [HBM] * 2 + [VM] * 6,
        out_specs=[VM] * 8,
        scratch_shapes=[
            VMEM((n_tok, width + 128), BF),
            VMEM((n_tok, width), BF),
            VMEM((q, width, f), BF),
            VMEM((nj, f, width), BF),
            VMEM((width, nj * f), BF),
            VMEM((width, q * f), BF),
            VMEM((q * f, width), BF),
            VMEM((n_tok, q * f), F32),
            VMEM((4 * rows, nj * f), F32),
            VMEM((n_tok, nj * f), BF),
            VMEM((n_tok, q * f), BF),
            VMEM((q, 1, f), F32),
            VMEM((q, 1, f), F32),
            VMEM((q, 8, f), F32),
            VMEM((q * rank, width), F32),
            VMEM((q * rank, width), F32),
            VMEM(mom.shape, F32),
            VMEM((q * rank, n_tok), F32),
            VMEM((q * rank, n_tok), F32),
            VMEM((n_tok, width), BF),
            VMEM((n_tok, width), BF),
            VMEM((4, nz * 2, rows // 2, width), BF),
            VMEM((4, nz, rows // 2, width), BF),
            VMEM((4, nz, rows // 2, width), BF),
            VMEM((4, nz, rows // 2, width), BF),
            VMEM((4, nz + 1, rows // 2, width), BF),
            DMA((q + 1,)),
            DMA((4, 5 * nz + 1)),
            DMA((4, n)),
            DMA((4, nz * 2)),
            DMA((4, nz * 2)),
            DMA((4, nz)),
            DMA((4, nz)),
            DMA((4, nz)),
            DMA((4, nz + 1)),
            DMA((2,)),
            DMA((2,)),
            DMA((4,)),
            DMA((4,)),
            VMEM((4, rows // 2, width), BF),
        ],
        compiler_params=pltpu.CompilerParams(
            collective_id=2, has_side_effects=True, vmem_limit_bytes=58 << 20
        ),
    )(tok, cot, ids, gates, w, wd, fin, fout, gains, mom, out_mom, gain_mom)
    return pl.pallas_call(
        place_kernel,
        out_shape=results,
        in_specs=[VM] * 8,
        out_specs=[VM] * 8,
    )(*made)


def mm(spec, a, b):
    return jnp.einsum(spec, a, b, preferred_element_type=F32)


def update(
    new_mom_all, out_grad, gain_grad, input_factor, output_factor, gains,
    in_moment, out_moment, gain_moment,
):
    new_in = input_factor - LEARN_RATE * new_mom_all
    share = in_moment.shape[3]
    new_in_moment = lax.dynamic_slice_in_dim(new_mom_all, lax.axis_index("dp") * share, share, 3)
    new_out_moment = MOMENTUM * out_moment + out_grad
    new_out = output_factor - LEARN_RATE * new_out_moment
    new_gain_moment = MOMENTUM * gain_moment + gain_grad
    new_gains = gains - LEARN_RATE * new_gain_moment
    return new_in, new_in_moment, new_out, new_out_moment, new_gains, new_gain_moment


def body(
    tokens,
    route_ids,
    route_slots,
    route_gates,
    out_cotangent,
    gate_up_weight,
    w_down,
    input_factor,
    output_factor,
    gains,
    in_moment,
    out_moment,
    gain_moment,
):
    n_expert = lax.axis_size("expert")
    experts_here = w_down.shape[0]
    experts_all = experts_here * n_expert
    tok_here, width = tokens.shape
    nz = n_expert // 2
    lanes = -(-experts_all // 128) * 128
    n_all = 4 * nz * tok_here
    if n_all <= 1024 and experts_all <= 64 and nz == PLAN_NZ and experts_here == 2:
        share = in_moment.shape[3]
        mixed, token_grad, new_in, new_mom, *rest = fused(
            nz, tokens, out_cotangent, route_ids.T, route_gates.T, gate_up_weight, w_down,
            input_factor, output_factor, gains, in_moment.reshape(-1, share), out_moment,
            gain_moment,
        )
        return (mixed, token_grad, new_in, new_mom.reshape(in_moment.shape), *rest)
    x, c, g, merged, norm2 = gather(
        nz, tokens, out_cotangent, route_ids, route_gates, gate_up_weight,
        input_factor, output_factor, gains, lanes,
    )
    x = x.reshape(n_all, width)
    c = c.reshape(n_all, width)
    moment_all = lax.all_gather(in_moment, "dp", axis=3, tiled=True)
    norm2 = norm2[:, :, 0]
    col_norm = jnp.sqrt(norm2)
    col_scale = gains / col_norm
    moment_all = lax.all_gather(in_moment, "dp", axis=3, tiled=True)

    i_hi = input_factor.astype(BF)
    start = lax.axis_index("expert") * experts_here
    gate = lax.dynamic_slice_in_dim(g.reshape(n_all, lanes), start, experts_here, 1)
    gate = gate.T[:, :, None]

    projected = mm("td,jpdf->jptf", x, merged)
    gate_pre = projected[:, 0]
    up_pre = projected[:, 1]
    s = jax.nn.sigmoid(gate_pre)
    hidden = (gate_pre * s * up_pre * gate).astype(BF)
    grad_hidden = mm("td,jfd->jtf", c, w_down) * gate
    grad_gate = (grad_hidden * up_pre * s * (1.0 + gate_pre * (1.0 - s))).astype(BF)
    grad_up = (grad_hidden * gate_pre * s).astype(BF)
    grad_pair = jnp.stack([grad_gate, grad_up], axis=1)
    part_mixed = mm("jtf,jfd->td", hidden, w_down).astype(BF)
    part_grad = mm("jptf,jpdf->td", grad_pair, merged).astype(BF)
    split = (4 * nz, tok_here, width)
    mixed, token_grad = scatter(nz, part_mixed.reshape(split), part_grad.reshape(split))

    act_sum = jnp.sum(grad_pair.astype(F32) * projected, axis=2)
    gain_grad = act_sum / gains
    curvature = act_sum / norm2
    scaled_out = output_factor * col_scale[:, :, None, :]
    tilted = output_factor * (curvature / col_scale)[:, :, None, :]
    t_rows = mm("jptf,jprf->jptr", grad_pair, scaled_out.astype(BF))
    in_part = ADAPTER_SCALE * (
        mm("jptr,td->jprd", t_rows.astype(BF), x)
        - mm("jprf,jpdf->jprd", tilted.astype(BF), merged)
    )
    low_rows = mm("td,jprd->jptr", x, i_hi)
    out_grad = ADAPTER_SCALE * (
        mm("jptr,jptf->jprf", low_rows.astype(BF), grad_pair) * col_scale[:, :, None, :]
        - mm("jprd,jpdf->jprf", i_hi, merged) * (curvature / col_scale)[:, :, None, :]
    )
    n_dp = lax.axis_size("dp")
    mine = in_part
    pieces = lax.all_gather(mine, "dp", axis=0)
    in_grad = pieces[0]
    for k in range(1, n_dp):
        in_grad = in_grad + pieces[k]
    new_mom_all = MOMENTUM * moment_all + in_grad
    return (mixed, token_grad) + update(
        new_mom_all, out_grad, gain_grad, input_factor, output_factor, gains,
        in_moment, out_moment, gain_moment,
    )


def solution(mesh):
    return jax.shard_map(
        body,
        mesh=mesh,
        in_specs=(
            P(("groups", "expert", "dp"), None),
            P(("groups", "expert", "dp"), None),
            P(("groups", "expert", "dp"), None),
            P(("groups", "expert", "dp"), None),
            P(("groups", "expert", "dp"), None),
            P("expert", None, None, "dp"),
            P("expert", "dp", None),
            P("expert", None, None, None),
            P("expert", None, None, "dp"),
            P("expert", None, "dp"),
            P("expert", None, None, "dp"),
            P("expert", None, None, "dp"),
            P("expert", None, "dp"),
        ),
        out_specs=(
            P(("groups", "expert", "dp"), None),
            P(("groups", "expert", "dp"), None),
            P(("groups", "expert"), None, None, None),
            P(("groups", "expert"), None, None, "dp"),
            P(("groups", "expert"), None, None, "dp"),
            P(("groups", "expert"), None, None, "dp"),
            P(("groups", "expert"), None, "dp"),
            P(("groups", "expert"), None, "dp"),
        ),
        check_vma=False,
    )
```

```python
import functools

import jax
import jax.numpy as jnp
from jax import lax
from jax.experimental import pallas as pl
from jax.experimental.pallas import tpu as pltpu
from jax.sharding import PartitionSpec as P

ADAPTER_SCALE = 2.0
MOMENTUM = 0.9
LEARN_RATE = 0.05
NORM_EPS = 1e-06
BF = jnp.bfloat16
F32 = jnp.float32


MESH = pl.DeviceIdType.MESH


def place():
    e = lax.axis_index("expert")
    return lax.div(e, 2), lax.rem(e, 2), lax.axis_index("dp")


def near(z, y, c, nz):
    return (
        (z < nz - 1, {"expert": (z + 1) * 2 + y}),
        (z > 0, {"expert": (z - 1) * 2 + y}),
        (None, {"expert": z * 2 + 1 - y}),
        (None, {"dp": 1 - c}),
    )


def when(cond, fn):
    if cond is None:
        fn()
    else:
        pl.when(cond)(fn)


def hail(z, y, c, nz):
    barrier = pltpu.get_barrier_semaphore()
    for cond, dev in near(z, y, c, nz):
        when(
            cond,
            lambda dev=dev: pl.semaphore_signal(barrier, 1, device_id=dev, device_id_type=MESH),
        )
    inner = jnp.logical_and(z > 0, z < nz - 1)
    return lambda: pl.semaphore_wait(barrier, 3 + inner.astype(jnp.int32))


def greet(z, y, c, nz):
    hail(z, y, c, nz)()


def gather_kernel(
    nz, tok, cot, ids, gates, w, fin, fout, gains, xo, co, go, merged, norm, wide, ssem, rsem
):
    z, y, c = place()
    right, left, across, twin = near(z, y, c, nz)
    outs = (xo, co, go)

    def idx(zz, yy, cc):
        return (zz * 2 + yy) * 2 + cc

    def copy(a, shard, dev, slot):
        return pltpu.make_async_remote_copy(
            src_ref=outs[a].at[shard],
            dst_ref=outs[a].at[shard],
            send_sem=ssem.at[a, slot],
            recv_sem=rsem.at[a, shard],
            device_id=dev,
            device_id_type=MESH,
        )

    def send(shard, dev, slot):
        for a in range(3):
            copy(a, shard, dev, slot).start()

    def got(shard):
        for a in range(3):
            copy(a, shard, twin[1], 0).wait_recv()

    def sent(shard, dev, slot):
        for a in range(3):
            copy(a, shard, dev, slot).wait_send()

    me = idx(z, y, c)
    xo[me] = tok[...]
    co[me] = cot[...]
    rows = tok.shape[0]
    lanes = go.shape[2]
    col = lax.broadcasted_iota(jnp.int32, (rows, lanes), 1)
    dense = jnp.zeros((rows, lanes), F32)
    for k in range(ids.shape[1]):
        dense = dense + jnp.where(col == ids[:, k : k + 1], gates[:, k : k + 1], 0.0)
    go[me] = dense
    greet(z, y, c, nz)

    prep = [(j, p) for j in range(w.shape[0]) for p in range(w.shape[1])]

    def prepare():
        if not prep:
            return
        j, p = prep.pop(0)
        fi = fin[j, p]
        fo = fout[j, p]
        ih = fi.astype(BF)
        il = (fi - ih.astype(F32)).astype(BF)
        oh = fo.astype(BF)
        ol = (fo - oh.astype(F32)).astype(BF)
        lhs = jnp.concatenate([ih, ih, il, il], axis=0)
        rhs = jnp.concatenate([oh, ol, oh, ol], axis=0)
        width = w.shape[2]
        tile = 256
        total = jnp.zeros((1, w.shape[3]), F32)
        for t in range(width // tile):
            low = lax.dot_general(
                lhs[:, t * tile : (t + 1) * tile],
                rhs,
                (((0,), (0,)), ((), ())),
                preferred_element_type=F32,
            )
            part = w[j, p, pl.ds(t * tile, tile), :].astype(F32) + ADAPTER_SCALE * low
            wide[pl.ds(t * tile, tile), :] = part
            total = total + jnp.sum(part * part, axis=0, keepdims=True)
        total = total + NORM_EPS
        norm[j, p] = total
        scale = gains[j, p : p + 1] / jnp.sqrt(total)
        for t in range(width // tile):
            merged[j, p, pl.ds(t * tile, tile), :] = (
                wide[pl.ds(t * tile, tile), :] * scale
            ).astype(BF)

    def step_z(s):
        def from_left():
            shard = idx(z - s, y, c)
            if s:
                got(shard)
            when(right[0], lambda: send(shard, right[1], z - s))
            if not s:
                when(left[0], lambda: send(shard, left[1], nz + z))
            send(shard, across[1], 2 * nz + z - s)
            send(shard, twin[1], 3 * nz + (z - s) * 2 + y)

        def from_right():
            shard = idx(z + s, y, c)
            got(shard)
            when(left[0], lambda: send(shard, left[1], nz + z + s))
            send(shard, across[1], 2 * nz + z + s)
            send(shard, twin[1], 3 * nz + (z + s) * 2 + y)

        if s == 0:
            from_left()
        else:
            pl.when(z - s >= 0)(from_left)
            pl.when(z + s < nz)(from_right)

    def step_y(s):
        def one(zz):
            shard = idx(zz, 1 - y, c)
            got(shard)
            send(shard, twin[1], 3 * nz + zz * 2 + 1 - y)

        if s == 0:
            one(z)
        else:
            pl.when(z - s >= 0)(lambda: one(z - s))
            pl.when(z + s < nz)(lambda: one(z + s))

    step_z(0)
    prepare()
    for s in range(1, nz):
        step_z(s)
        step_y(s - 1)
        prepare()
    step_y(nz - 1)
    while prep:
        prepare()
    for zz in range(nz):
        for yy in range(2):
            got(idx(zz, yy, 1 - c))
    for zz in range(nz):
        here = z >= zz
        pl.when(jnp.logical_and(here, z < nz - 1))(
            lambda: sent(idx(zz, y, c), right[1], zz)
        )
        there = z <= zz
        pl.when(jnp.logical_and(there, z > 0))(
            lambda: sent(idx(zz, y, c), left[1], nz + zz)
        )
        sent(idx(zz, y, c), across[1], 2 * nz + zz)
        for yy in range(2):
            sent(idx(zz, yy, c), twin[1], 3 * nz + zz * 2 + yy)


def scatter_kernel(nz, pa, pb, oa, ob, rd, ys, ry, zs, rz, dss, drs, yss, yrs, zss, zrs):
    z, y, c = place()
    right, left, across, twin = near(z, y, c, nz)
    parts = (pa, pb)
    outs = (oa, ob)

    def idx(zz, yy, cc):
        return (zz * 2 + yy) * 2 + cc

    def remote(src, dst, a, b, dev):
        return pltpu.make_async_remote_copy(
            src_ref=src, dst_ref=dst, send_sem=a, recv_sem=b, device_id=dev, device_id_type=MESH
        )

    def to_twin(m, zz, yy):
        k = zz * 2 + yy
        return remote(
            parts[m].at[idx(zz, yy, 1 - c)], rd.at[m, k], dss.at[m, k], drs.at[m, k], twin[1]
        )

    def to_across(m, zz):
        return remote(ys.at[m, zz], ry.at[m, zz], yss.at[m, zz], yrs.at[m, zz], across[1])

    def to_right(m, zz):
        return remote(
            zs.at[m, zz], rz.at[m, zz + 1], zss.at[m, zz], zrs.at[m, zz + 1], right[1]
        )

    def to_left(m, zz):
        return remote(zs.at[m, zz], rz.at[m, zz], zss.at[m, zz], zrs.at[m, zz], left[1])

    def wide(v):
        return v.astype(F32)

    greet(z, y, c, nz)

    def each(s, fn):
        if s == 0:
            fn(z)
        else:
            pl.when(z + s < nz)(lambda: fn(z + s))
            pl.when(z - s >= 0)(lambda: fn(z - s))

    order = list(range(nz - 1, -1, -1))
    for m in range(2):
        for s in order:
            each(s, lambda zz: to_twin(m, zz, 1 - y).start())
        for s in order:
            each(s, lambda zz: to_twin(m, zz, y).start())

    def y_part(m, s):
        def one(zz):
            to_twin(m, zz, 1 - y).wait_recv()
            ys[m, zz] = (
                wide(parts[m][idx(zz, 1 - y, c)]) + wide(rd[m, zz * 2 + 1 - y])
            ).astype(BF)
            to_across(m, zz).start()

        each(s, one)

    def held(m, zz):
        to_twin(m, zz, y).wait_recv()
        to_across(m, zz).wait_recv()
        return wide(parts[m][idx(zz, y, c)]) + wide(rd[m, zz * 2 + y]) + wide(ry[m, zz])

    def z_part(m, s):
        def rightward():
            zz = z + s
            zs[m, zz] = held(m, zz).astype(BF)

            @pl.when(z > 0)
            def _():
                to_right(m, zz).wait_recv()
                zs[m, zz] = (wide(zs[m, zz]) + wide(rz[m, zz + 1])).astype(BF)

            to_right(m, zz).start()

        def leftward():
            zz = z - s
            zs[m, zz] = held(m, zz).astype(BF)

            @pl.when(z < nz - 1)
            def _():
                to_left(m, zz).wait_recv()
                zs[m, zz] = (wide(zs[m, zz]) + wide(rz[m, zz])).astype(BF)

            to_left(m, zz).start()

        pl.when(z + s < nz)(rightward)
        pl.when(z - s >= 0)(leftward)

    for m in range(2):
        for s in order:
            y_part(m, s)
    for m in range(2):
        for s in order[:-1]:
            z_part(m, s)
        zs[m, z] = held(m, z).astype(BF)

        @pl.when(z > 0)
        def _():
            to_right(m, z).wait_recv()
            zs[m, z] = (wide(zs[m, z]) + wide(rz[m, z + 1])).astype(BF)

        @pl.when(z < nz - 1)
        def _():
            to_left(m, z).wait_recv()
            zs[m, z] = (wide(zs[m, z]) + wide(rz[m, z])).astype(BF)

        outs[m][...] = zs[m, z]
    for m in range(2):
        for zz in range(nz):
            for yy in range(2):
                to_twin(m, zz, yy).wait_send()
            to_across(m, zz).wait_send()
            pl.when(z < zz)(lambda: to_right(m, zz).wait_send())
            pl.when(z > zz)(lambda: to_left(m, zz).wait_send())


GATHER_BYPASS = (False, True, True, True)
SCATTER_BYPASS = (True, True, False, True)
PLAN_NZ = 4
PLAN = (
    (1, "z", 0, 1), (0, "z", 5, 0), (0, "z", 0, 1), (1, "z", 0, 0), (2, "p", 3),
    (0, "z", 0, 0), (2, "t"), (1, "z", 0, 2), (0, "z", 0, 2), (0, "z", 5, 1), (1, "z", 1, 1),
    (1, "z", 1, 0), (1, "y", 0, 1), (2, "p", 0), (1, "y", 0, 0), (1, "z", 0, 3),
    (0, "z", 0, 3), (2, "p", 2), (1, "z", 2, 1), (2, "p", 1), (0, "y", 0, 0), (2, "m"),
    (0, "z", 1, 1), (1, "z", 2, 0), (0, "z", 1, 0), (1, "z", 4, 0), (1, "z", 1, 2),
    (0, "y", 0, 1), (2, "U", 0), (0, "z", 2, 1), (1, "z", 1, 3), (1, "z", 2, 2),
    (0, "y", 0, 2), (1, "y", 0, 2), (1, "y", 1, 0), (0, "y", 0, 3), (1, "y", 0, 3),
    (2, "V", 0), (1, "y", 2, 0), (0, "y", 1, 0), (1, "y", 1, 1), (0, "z", 2, 0),
    (1, "z", 3, 1), (1, "z", 3, 0), (0, "y", 1, 1), (2, "U", 1), (0, "z", 3, 1),
    (1, "y", 2, 1), (1, "z", 2, 3), (1, "y", 3, 0), (1, "z", 4, 1), (0, "y", 2, 1),
    (2, "D", 0), (1, "z", 3, 2), (0, "y", 2, 0), (2, "D", 1), (0, "z", 3, 0), (0, "z", 1, 2),
    (0, "z", 1, 3), (2, "U", 2), (0, "z", 2, 2), (1, "y", 1, 2), (0, "z", 2, 3),
    (1, "y", 1, 3), (0, "Y", 1, 1), (1, "y", 3, 1), (1, "z", 5, 0), (2, "D", 2),
    (0, "y", 3, 1), (0, "y", 3, 0), (0, "Y", 0, 1), (1, "y", 2, 2), (0, "Z", 1, 1),
    (0, "z", 3, 2), (2, "U", 3), (2, "D", 3), (1, "Y", 0, 3), (1, "Y", 0, 2), (1, "y", 2, 3),
    (0, "Y", 1, 3), (0, "Y", 0, 3), (0, "y", 1, 3), (0, "y", 1, 2), (0, "y", 2, 2),
    (0, "y", 2, 3), (1, "z", 3, 3), (1, "Y", 1, 3), (2, "V", 2), (1, "Y", 0, 1),
    (1, "y", 3, 3), (0, "z", 3, 3), (2, "V", 1), (0, "Y", 1, 2), (2, "W", 2), (0, "Z", 1, 3),
    (0, "y", 3, 2), (1, "Y", 2, 2), (1, "Y", 1, 1), (0, "Y", 2, 2), (0, "Z", 0, 3),
    (0, "z", 4, 0), (0, "Y", 0, 2), (0, "y", 3, 3), (1, "y", 3, 2), (1, "Y", 1, 2),
    (2, "V", 3), (2, "W", 3), (0, "Z", 2, 2), (1, "Y", 1, 0), (0, "Y", 3, 3), (0, "Y", 2, 3),
    (0, "Y", 3, 2), (1, "Z", 0, 3), (0, "Z", 1, 2), (1, "Y", 3, 3), (1, "Z", 1, 3),
    (1, "Y", 2, 3), (2, "x"), (1, "Y", 3, 2), (0, "Z", 0, 2), (0, "Y", 1, 0), (2, "W", 1),
    (0, "Z", 3, 3), (1, "Z", 0, 1), (2, "x"), (0, "Y", 2, 1), (0, "Z", 2, 3), (1, "Z", 1, 2),
    (1, "Y", 3, 1), (1, "Y", 0, 0), (1, "Z", 3, 3), (2, "x"), (0, "Z", 3, 2), (1, "Y", 2, 1),
    (1, "z", 5, 1), (1, "Z", 2, 3), (0, "Y", 3, 1), (1, "Z", 0, 2), (0, "Z", 3, 1),
    (0, "Z", 0, 1), (1, "Z", 1, 1), (2, "W", 0), (0, "Y", 2, 0), (1, "Y", 2, 0),
    (0, "Z", 2, 1), (1, "Z", 3, 2), (1, "Z", 3, 1), (0, "Y", 3, 0), (2, "x"), (0, "Y", 0, 0),
    (1, "Z", 2, 2), (1, "Y", 3, 0), (2, "x"), (1, "Z", 2, 1), (2, "x"), (1, "E", 0),
    (0, "E", 0), (0, "E", 1), (2, "x"), (0, "E", 3), (0, "E", 2), (1, "E", 3), (1, "E", 1),
    (1, "E", 2), (0, "z", 4, 1),
)


def fused_kernel(
    nz, tok, cot, ids, gates, w, wd_in, fin, fout, gains, mom, out_mom, gain_mom,
    mixed, token_grad, new_in, new_mom, new_out, new_out_mom, new_gain, new_gain_mom,
    xg, cg, wv, wd, wdt, cm, cmt, pr, gh, hid, gp, norm, scl, act, inp, rin, rmom, lowt, tt,
    pa, pb, rd, ys, ry, zs, rz,
    lsem, gss, grs, dss, drs, yss, yrs, zss, zrs, ess, ers, pss, prs, rp,
):
    z, y, c = place()
    right, left, across, twin = near(z, y, c, nz)
    pz = z + 1 - 2 * lax.rem(z, 2)
    partner = {"expert": pz * 2 + y}
    heard = hail(z, y, c, nz)
    parts = (pa, pb)
    outs = (mixed, token_grad)
    rows, width = tok.shape
    nj, _, rank, f = fout.shape
    npair = 2 * nj
    slab = 4 * rows

    def idx(zz, yy, cc):
        return (zz * 2 + yy) * 2 + cc

    def dot(u, v):
        return jnp.dot(u, v, preferred_element_type=F32)

    def dot_nt(u, v):
        return lax.dot_general(u, v, (((1,), (1,)), ((), ())), preferred_element_type=F32)

    def wide(v):
        return v.astype(F32)

    def at(shard):
        return pl.ds(pl.multiple_of(shard * rows, rows), rows)

    hr = rows // 2

    def at_half(shard, m):
        return pl.ds(pl.multiple_of(shard * rows + (m % 2) * hr, hr), hr)

    def remote(src, dst, a, b, dev):
        return pltpu.make_async_remote_copy(
            src_ref=src, dst_ref=dst, send_sem=a, recv_sem=b, device_id=dev, device_id_type=MESH
        )

    loads = [
        pltpu.make_async_copy(w.at[q // 2, q % 2], wv.at[q], lsem.at[q]) for q in range(npair)
    ]
    load_down = pltpu.make_async_copy(wd_in, wd, lsem.at[npair])
    for load in loads:
        load.start()
    load_down.start()

    me = idx(z, y, c)
    half = (xg.shape[1] - width) // 2
    row = lax.broadcasted_iota(jnp.int32, (half, rows), 0)
    dense = jnp.zeros((half, rows), F32)
    for k in range(ids.shape[0]):
        dense = dense + jnp.where(row == ids[k : k + 1, :], gates[k : k + 1, :], 0.0)
    high = dense.astype(BF)
    both = jnp.concatenate([high, (dense - wide(high)).astype(BF)], axis=0)
    eye = (
        lax.broadcasted_iota(jnp.int32, (rows, rows), 0)
        == lax.broadcasted_iota(jnp.int32, (rows, rows), 1)
    ).astype(BF)
    xg[at(me), pl.ds(0, width)] = tok[...]
    xg[at(me), pl.ds(width, 2 * half)] = dot_nt(eye, both).astype(BF)
    cg[at(me), :] = cot[...]

    held_rows = (xg, cg)

    def gcopy(a, shard, dev, s):
        ref = held_rows[a // 2].at[at_half(shard, a), :]
        return remote(ref, ref, gss.at[a, s], grs.at[a, shard], dev)

    def got(a, shard):
        gcopy(a, shard, twin[1], 0).wait_recv()

    def cross(a, s, zz):
        send = gcopy(a, idx(zz, y, c), across[1], 2 * nz + zz)
        if GATHER_BYPASS[a] and s == 1:
            pl.when(zz != pz)(lambda: send.start())
        else:
            send.start()

    def z_step(s, a):
        def from_left():
            shard = idx(z - s, y, c)
            if s:
                got(a, shard)
            when(right[0], lambda: gcopy(a, shard, right[1], z - s).start())
            if not s:
                when(left[0], lambda: gcopy(a, shard, left[1], nz + z).start())
            cross(a, s, z - s)
            gcopy(a, shard, twin[1], 3 * nz + (z - s) * 2 + y).start()

        def from_right():
            shard = idx(z + s, y, c)
            got(a, shard)
            when(left[0], lambda: gcopy(a, shard, left[1], nz + z + s).start())
            cross(a, s, z + s)
            gcopy(a, shard, twin[1], 3 * nz + (z + s) * 2 + y).start()

        if s == 0:
            from_left()
        elif s < nz:
            pl.when(z - s >= 0)(from_left)
            pl.when(z + s < nz)(from_right)

    def y_step(s, a):
        def one(zz):
            shard = idx(zz, 1 - y, c)
            got(a, shard)
            gcopy(a, shard, twin[1], 3 * nz + zz * 2 + 1 - y).start()

        if s == 0:
            one(z)
            if GATHER_BYPASS[a]:
                gcopy(a, idx(z, 1 - y, c), partner, 5 * nz).start()
        elif s < nz:
            pl.when(z - s >= 0)(lambda: one(z - s))
            pl.when(z + s < nz)(lambda: one(z + s))

    def slot(k):
        m = jnp.minimum(z, nz - 1 - z)
        close = z - (k + 1) // 2 if k % 2 else z + k // 2
        far = jnp.where(2 * z < nz - 1, z + (k - m), z - (k - m))
        return jnp.where(k <= 2 * m, close, far)

    def to_twin(m, zz, yy):
        k = zz * 2 + yy
        return remote(
            parts[m // 2].at[at_half(idx(zz, yy, 1 - c), m), :],
            rd.at[m, k],
            dss.at[m, k],
            drs.at[m, k],
            twin[1],
        )

    def to_across(m, zz):
        return remote(ys.at[m, zz], ry.at[m, zz], yss.at[m, zz], yrs.at[m, zz], across[1])

    def to_right(m, zz):
        return remote(
            zs.at[m, zz], rz.at[m, zz + 1], zss.at[m, zz], zrs.at[m, zz + 1], right[1]
        )

    def to_left(m, zz):
        return remote(zs.at[m, zz], rz.at[m, zz], zss.at[m, zz], zrs.at[m, zz], left[1])

    def to_partner(m):
        return remote(ys.at[m, pz], rp.at[m], pss.at[m], prs.at[m], partner)

    def y_part(m, k):
        zz = slot(k)
        to_twin(m, zz, 1 - y).wait_recv()
        part = wide(parts[m // 2][at_half(idx(zz, 1 - y, c), m), :]) + wide(
            rd[m, zz * 2 + 1 - y]
        )
        if k == 0 and SCATTER_BYPASS[m]:
            to_partner(m).wait_recv()
            part = part + wide(rp[m])
        ys[m, zz] = part.astype(BF)
        if k == 0 or not SCATTER_BYPASS[m]:
            to_across(m, zz).start()
        else:
            pl.when(zz != pz)(lambda: to_across(m, zz).start())
            pl.when(zz == pz)(lambda: to_partner(m).start())

    def own(m, zz):
        return wide(parts[m // 2][at_half(idx(zz, y, c), m), :]) + wide(rd[m, zz * 2 + y])

    def held(m, zz):
        to_across(m, zz).wait_recv()
        return own(m, zz) + wide(ry[m, zz])

    def z_part(m, k):
        zz = slot(k)
        to_twin(m, zz, y).wait_recv()
        if SCATTER_BYPASS[m]:

            @pl.when(zz != pz)
            def _():
                zs[m, zz] = held(m, zz).astype(BF)

            @pl.when(zz == pz)
            def _():
                zs[m, zz] = own(m, zz).astype(BF)

        else:
            zs[m, zz] = held(m, zz).astype(BF)

        @pl.when(zz > z)
        def _():
            @pl.when(z > 0)
            def _():
                to_right(m, zz).wait_recv()
                zs[m, zz] = (wide(zs[m, zz]) + wide(rz[m, zz + 1])).astype(BF)

            to_right(m, zz).start()

        @pl.when(zz < z)
        def _():
            @pl.when(z < nz - 1)
            def _():
                to_left(m, zz).wait_recv()
                zs[m, zz] = (wide(zs[m, zz]) + wide(rz[m, zz])).astype(BF)

            to_left(m, zz).start()

    def finish(m):
        to_twin(m, z, y).wait_recv()
        zs[m, z] = held(m, z).astype(BF)

        @pl.when(z > 0)
        def _():
            to_right(m, z).wait_recv()
            zs[m, z] = (wide(zs[m, z]) + wide(rz[m, z + 1])).astype(BF)

        @pl.when(z < nz - 1)
        def _():
            to_left(m, z).wait_recv()
            zs[m, z] = (wide(zs[m, z]) + wide(rz[m, z])).astype(BF)

        outs[m // 2][pl.ds((m % 2) * hr, hr), :] = zs[m, z]

    def cols(q):
        return pl.ds(q * f, f)

    def prepare(q):
        loads[q].wait()
        fi = fin[q // 2, q % 2]
        fo = fout[q // 2, q % 2]
        ih = fi.astype(BF)
        il = (fi - wide(ih)).astype(BF)
        oh = fo.astype(BF)
        ol = (fo - wide(oh)).astype(BF)
        lhs = jnp.concatenate([ih, ih, il, il], axis=0)
        rhs = jnp.concatenate([oh, ol, oh, ol], axis=0)
        tile = 256
        total = jnp.zeros((8, f), F32)
        for t in range(width // tile):
            low = lax.dot_general(
                lhs[:, t * tile : (t + 1) * tile],
                rhs,
                (((0,), (0,)), ((), ())),
                preferred_element_type=F32,
            )
            part = wide(wv[q, pl.ds(t * tile, tile), :]) + ADAPTER_SCALE * low
            cm[pl.ds(t * tile, tile), cols(q)] = part.astype(BF)
            cmt[cols(q), pl.ds(t * tile, tile)] = part.astype(BF).T
            total = total + jnp.sum((part * part).reshape(tile // 8, 8, f), axis=0)
        total = jnp.sum(total, axis=0, keepdims=True) + NORM_EPS
        norm[q] = total
        scl[q] = gains[q // 2, q % 2 : q % 2 + 1] / jnp.sqrt(total)
        act[q] = jnp.zeros((8, f), F32)

    def turn_down():
        load_down.wait()
        for j in range(nj):
            for t in range(width // 256):
                wdt[pl.ds(t * 256, 256), pl.ds(j * f, f)] = wd[j, :, pl.ds(t * 256, 256)].T

    start = lax.axis_index("expert") * nj
    tile = 32
    lane = lax.broadcasted_iota(jnp.int32, (tile, 2 * half), 1)

    def gate_of(r, j):
        g = wide(xg[r, pl.ds(width, 2 * half)])
        mine = (lane == start + j) | (lane == start + j + half)
        return jnp.sum(jnp.where(mine, g, 0.0), axis=1, keepdims=True)

    def rise(k):
        zz = slot(k)
        base = zz * slab
        r = pl.ds(pl.multiple_of(base, slab), slab)
        for yy in range(2):
            got(0, idx(zz, yy, 1 - c))
            got(1, idx(zz, yy, 1 - c))
        for j in range(nj):
            n = pl.ds(j * 2 * f, 2 * f)
            pr[r, n] = dot(xg[r, pl.ds(0, width)], cm[:, n])

        def gating(i, _):
            t = pl.ds(pl.multiple_of(base + i * tile, tile), tile)
            for j in range(nj):
                pre = pr[t, cols(2 * j)] * scl[2 * j]
                up = pr[t, cols(2 * j + 1)] * scl[2 * j + 1]
                hid[t, cols(j)] = (pre * jax.nn.sigmoid(pre) * up * gate_of(t, j)).astype(BF)
            return 0

        lax.fori_loop(0, slab // tile, gating, 0)

    def fall(k):
        zz = slot(k)
        r = pl.ds(pl.multiple_of(zz * slab, slab), slab)
        for t in range(width // 512):
            n = pl.ds(t * 512, 512)
            acc = dot(hid[r, cols(0)], wd[0, :, n])
            for j in range(1, nj):
                acc = acc + dot(hid[r, cols(j)], wd[j, :, n])
            pa[r, n] = acc.astype(BF)
        for yy in range(2):
            to_twin(0, zz, yy).start()
            to_twin(1, zz, yy).start()

    def bend(k):
        zz = slot(k)
        base = zz * slab
        r = pl.ds(pl.multiple_of(base, slab), slab)
        for yy in range(2):
            got(2, idx(zz, yy, 1 - c))
            got(3, idx(zz, yy, 1 - c))
        gh[...] = dot(cg[r, :], wdt[...])

        def gating(i, _):
            t = pl.ds(pl.multiple_of(base + i * tile, tile), tile)
            here = pl.ds(pl.multiple_of(i * tile, tile), tile)
            for j in range(nj):
                raw0 = pr[t, cols(2 * j)]
                raw1 = pr[t, cols(2 * j + 1)]
                s0 = scl[2 * j]
                s1 = scl[2 * j + 1]
                pre = raw0 * s0
                up = raw1 * s1
                s = jax.nn.sigmoid(pre)
                gr = gh[here, cols(j)] * gate_of(t, j)
                g0 = (gr * up * s * (1.0 + pre * (1.0 - s)) * s0).astype(BF)
                g1 = (gr * pre * s * s1).astype(BF)
                gp[t, cols(2 * j)] = g0
                gp[t, cols(2 * j + 1)] = g1
                for q, g, raw in ((2 * j, g0, raw0), (2 * j + 1, g1, raw1)):
                    term = wide(g) * raw
                    act[q] += jnp.sum(term.reshape(tile // 8, 8, f), axis=0)
            return 0

        lax.fori_loop(0, slab // tile, gating, 0)

    def back(k):
        zz = slot(k)
        r = pl.ds(pl.multiple_of(zz * slab, slab), slab)
        for t in range(width // 512):
            n = pl.ds(t * 512, 512)
            acc = dot(gp[r, pl.ds(0, 2 * f)], cmt[pl.ds(0, 2 * f), n])
            for j in range(1, nj):
                k2 = pl.ds(j * 2 * f, 2 * f)
                acc = acc + dot(gp[r, k2], cmt[k2, n])
            pb[r, n] = acc.astype(BF)
        for yy in range(2):
            to_twin(2, zz, yy).start()
            to_twin(3, zz, yy).start()

    group = [pl.ds(q * rank, rank) for q in range(npair)]

    def low_in():
        ih = jnp.concatenate([fin[q // 2, q % 2] for q in range(npair)], axis=0).astype(BF)
        lowt[...] = dot_nt(ih, xg[:, pl.ds(0, width)])

    def low_out():
        for q in range(npair):
            tt[group[q], :] = dot_nt(fout[q // 2, q % 2].astype(BF), gp[:, cols(q)])
        inp[...] = dot(tt[...].astype(BF), xg[:, pl.ds(0, width)])

    def total_act(q):
        return jnp.sum(act[q], axis=0, keepdims=True)

    def in_part():
        for q in range(npair):
            curved = fout[q // 2, q % 2] * (total_act(q) / norm[q])
            low = dot(curved.astype(BF), cmt[cols(q), :])
            inp[group[q], :] = ADAPTER_SCALE * (inp[group[q], :] - low)
        swap_inp.start()

    def out_part(q):
        j, p = q // 2, q % 2
        total = total_act(q)
        first = dot(lowt[group[q], :].astype(BF), gp[:, cols(q)])
        second = dot(fin[j, p].astype(BF), cm[:, cols(q)]) * (total / norm[q])
        moved = MOMENTUM * out_mom[j, p] + ADAPTER_SCALE * (first - second)
        new_out_mom[j, p] = moved
        new_out[j, p] = fout[j, p] - LEARN_RATE * moved
        one = pl.ds(p, 1)
        bent = MOMENTUM * gain_mom[j, one, :] + total / gains[j, one, :]
        new_gain_mom[j, one, :] = bent
        new_gain[j, one, :] = gains[j, one, :] - LEARN_RATE * bent

    def in_finish():
        swap_mom.wait()
        swap_inp.wait()
        share = mom.shape[1]
        for own in range(2):
            k = pl.ds(pl.multiple_of((c if own else 1 - c) * share, share), share)
            old = mom[...] if own else rmom[...]
            moved = MOMENTUM * old + (inp[:, k] + rin[:, k])
            if own:
                new_mom[...] = moved
            for q in range(npair):
                new_in[q // 2, q % 2, :, k] = (
                    fin[q // 2, q % 2, :, k]
                    - LEARN_RATE * moved[q * rank : (q + 1) * rank]
                )

    swap_mom = remote(mom, rmom, ess.at[0], ers.at[0], twin[1])
    swap_inp = remote(inp, rin, ess.at[1], ers.at[1], twin[1])

    heard()
    extra = [low_in, low_out, in_part] + [functools.partial(out_part, q) for q in range(npair)]

    def filler():
        if extra:
            extra.pop(0)()

    turns = {
        "z": z_step,
        "y": y_step,
        "p": prepare,
        "t": turn_down,
        "m": lambda: swap_mom.start(),
        "U": rise,
        "D": fall,
        "V": bend,
        "W": back,
        "Y": y_part,
        "Z": z_part,
        "E": finish,
        "x": filler,
    }
    edge = (z == 0) | (z == nz - 1)
    some = ([], [])

    def flush():
        def go(which):
            for name, *args in which:
                turns[name](*args)

        first, second = list(some[0]), list(some[1])
        while first and second and first[0] == second[0]:
            go([first.pop(0)])
            second.pop(0)
        if first:
            pl.when(edge)(functools.partial(go, first))
        if second:
            pl.when(jnp.logical_not(edge))(functools.partial(go, second))
        some[0].clear()
        some[1].clear()

    for tag, *turn in PLAN:
        if tag < 2:
            some[tag].append(tuple(turn))
        else:
            flush()
            turns[turn[0]](*turn[1:])
    flush()
    while extra:
        filler()
    in_finish()
    for a in range(4):
        for zz in range(nz):
            pl.when(jnp.logical_and(z >= zz, z < nz - 1))(
                lambda: gcopy(a, idx(zz, y, c), right[1], zz).wait_send()
            )
            pl.when(jnp.logical_and(z <= zz, z > 0))(
                lambda: gcopy(a, idx(zz, y, c), left[1], nz + zz).wait_send()
            )
            crossed = gcopy(a, idx(zz, y, c), across[1], 2 * nz + zz)
            if GATHER_BYPASS[a]:
                pl.when(pz != zz)(lambda: crossed.wait_send())
            else:
                crossed.wait_send()
            for yy in range(2):
                gcopy(a, idx(zz, yy, c), twin[1], 3 * nz + zz * 2 + yy).wait_send()
        if GATHER_BYPASS[a]:
            gcopy(a, idx(z, 1 - y, c), partner, 5 * nz).wait_send()
    for m in range(4):
        for zz in range(nz):
            for yy in range(2):
                to_twin(m, zz, yy).wait_send()
            if SCATTER_BYPASS[m]:
                pl.when(pz != zz)(lambda: to_across(m, zz).wait_send())
            else:
                to_across(m, zz).wait_send()
            pl.when(z < zz)(lambda: to_right(m, zz).wait_send())
            pl.when(z > zz)(lambda: to_left(m, zz).wait_send())
        if SCATTER_BYPASS[m]:
            to_partner(m).wait_send()


def place_kernel(*refs):
    n = len(refs) // 2
    for k in range(n):
        refs[n + k][...] = refs[k][...]


VM = pl.BlockSpec(memory_space=pltpu.VMEM)
HBM = pl.BlockSpec(memory_space=pl.ANY)
DMA = pltpu.SemaphoreType.DMA


def gather(nz, tok, cot, ids, gates, w, fin, fout, gains, lanes):
    n = nz * 4
    rows, width = tok.shape
    j, p, d, f = w.shape
    return pl.pallas_call(
        functools.partial(gather_kernel, nz),
        out_shape=(
            jax.ShapeDtypeStruct((n, rows, width), BF),
            jax.ShapeDtypeStruct((n, rows, width), BF),
            jax.ShapeDtypeStruct((n, rows, lanes), F32),
            jax.ShapeDtypeStruct(w.shape, BF),
            jax.ShapeDtypeStruct((j, p, 1, f), F32),
        ),
        in_specs=[VM] * 8,
        out_specs=[VM] * 5,
        scratch_shapes=[pltpu.VMEM((d, f), F32), DMA((3, 5 * nz)), DMA((3, n))],
        compiler_params=pltpu.CompilerParams(
            collective_id=0, has_side_effects=True, vmem_limit_bytes=56 << 20
        ),
    )(tok, cot, ids, gates, w, fin, fout, gains)


def scatter(nz, pa, pb):
    n, rows, width = pa.shape
    row = jax.ShapeDtypeStruct((rows, width), BF)
    return pl.pallas_call(
        functools.partial(scatter_kernel, nz),
        out_shape=(row, row),
        in_specs=[VM] * 2,
        out_specs=[VM] * 2,
        scratch_shapes=[
            pltpu.VMEM((2, nz * 2, rows, width), BF),
            pltpu.VMEM((2, nz, rows, width), BF),
            pltpu.VMEM((2, nz, rows, width), BF),
            pltpu.VMEM((2, nz, rows, width), BF),
            pltpu.VMEM((2, nz + 1, rows, width), BF),
            DMA((2, nz * 2)),
            DMA((2, nz * 2)),
            DMA((2, nz)),
            DMA((2, nz)),
            DMA((2, nz)),
            DMA((2, nz + 1)),
        ],
        compiler_params=pltpu.CompilerParams(
            collective_id=1, has_side_effects=True, vmem_limit_bytes=56 << 20
        ),
    )(pa, pb)


def fused(nz, tok, cot, ids, gates, w, wd, fin, fout, gains, mom, out_mom, gain_mom):
    rows, width = tok.shape
    n = 4 * nz
    n_tok = n * rows
    nj, _, rank, f = fout.shape
    q = 2 * nj
    VMEM = pltpu.VMEM
    shape = jax.ShapeDtypeStruct
    row = shape((rows, width), BF)
    results = (
        row,
        row,
        shape(fin.shape, F32),
        shape(mom.shape, F32),
        shape(fout.shape, F32),
        shape(fout.shape, F32),
        shape(gains.shape, F32),
        shape(gains.shape, F32),
    )
    made = pl.pallas_call(
        functools.partial(fused_kernel, nz),
        out_shape=results,
        in_specs=[VM] * 4 + [HBM] * 2 + [VM] * 6,
        out_specs=[VM] * 8,
        scratch_shapes=[
            VMEM((n_tok, width + 128), BF),
            VMEM((n_tok, width), BF),
            VMEM((q, width, f), BF),
            VMEM((nj, f, width), BF),
            VMEM((width, nj * f), BF),
            VMEM((width, q * f), BF),
            VMEM((q * f, width), BF),
            VMEM((n_tok, q * f), F32),
            VMEM((4 * rows, nj * f), F32),
            VMEM((n_tok, nj * f), BF),
            VMEM((n_tok, q * f), BF),
            VMEM((q, 1, f), F32),
            VMEM((q, 1, f), F32),
            VMEM((q, 8, f), F32),
            VMEM((q * rank, width), F32),
            VMEM((q * rank, width), F32),
            VMEM(mom.shape, F32),
            VMEM((q * rank, n_tok), F32),
            VMEM((q * rank, n_tok), F32),
            VMEM((n_tok, width), BF),
            VMEM((n_tok, width), BF),
            VMEM((4, nz * 2, rows // 2, width), BF),
            VMEM((4, nz, rows // 2, width), BF),
            VMEM((4, nz, rows // 2, width), BF),
            VMEM((4, nz, rows // 2, width), BF),
            VMEM((4, nz + 1, rows // 2, width), BF),
            DMA((q + 1,)),
            DMA((4, 5 * nz + 1)),
            DMA((4, n)),
            DMA((4, nz * 2)),
            DMA((4, nz * 2)),
            DMA((4, nz)),
            DMA((4, nz)),
            DMA((4, nz)),
            DMA((4, nz + 1)),
            DMA((2,)),
            DMA((2,)),
            DMA((4,)),
            DMA((4,)),
            VMEM((4, rows // 2, width), BF),
        ],
        compiler_params=pltpu.CompilerParams(
            collective_id=2, has_side_effects=True, vmem_limit_bytes=58 << 20
        ),
    )(tok, cot, ids, gates, w, wd, fin, fout, gains, mom, out_mom, gain_mom)
    return pl.pallas_call(
        place_kernel,
        out_shape=results,
        in_specs=[VM] * 8,
        out_specs=[VM] * 8,
    )(*made)


def mm(spec, a, b):
    return jnp.einsum(spec, a, b, preferred_element_type=F32)


def update(
    new_mom_all, out_grad, gain_grad, input_factor, output_factor, gains,
    in_moment, out_moment, gain_moment,
):
    new_in = input_factor - LEARN_RATE * new_mom_all
    share = in_moment.shape[3]
    new_in_moment = lax.dynamic_slice_in_dim(new_mom_all, lax.axis_index("dp") * share, share, 3)
    new_out_moment = MOMENTUM * out_moment + out_grad
    new_out = output_factor - LEARN_RATE * new_out_moment
    new_gain_moment = MOMENTUM * gain_moment + gain_grad
    new_gains = gains - LEARN_RATE * new_gain_moment
    return new_in, new_in_moment, new_out, new_out_moment, new_gains, new_gain_moment


def body(
    tokens,
    route_ids,
    route_slots,
    route_gates,
    out_cotangent,
    gate_up_weight,
    w_down,
    input_factor,
    output_factor,
    gains,
    in_moment,
    out_moment,
    gain_moment,
):
    n_expert = lax.axis_size("expert")
    experts_here = w_down.shape[0]
    experts_all = experts_here * n_expert
    tok_here, width = tokens.shape
    nz = n_expert // 2
    lanes = -(-experts_all // 128) * 128
    n_all = 4 * nz * tok_here
    if n_all <= 1024 and experts_all <= 64 and nz == PLAN_NZ and experts_here == 2:
        share = in_moment.shape[3]
        mixed, token_grad, new_in, new_mom, *rest = fused(
            nz, tokens, out_cotangent, route_ids.T, route_gates.T, gate_up_weight, w_down,
            input_factor, output_factor, gains, in_moment.reshape(-1, share), out_moment,
            gain_moment,
        )
        return (mixed, token_grad, new_in, new_mom.reshape(in_moment.shape), *rest)
    x, c, g, merged, norm2 = gather(
        nz, tokens, out_cotangent, route_ids, route_gates, gate_up_weight,
        input_factor, output_factor, gains, lanes,
    )
    x = x.reshape(n_all, width)
    c = c.reshape(n_all, width)
    moment_all = lax.all_gather(in_moment, "dp", axis=3, tiled=True)
    norm2 = norm2[:, :, 0]
    col_norm = jnp.sqrt(norm2)
    col_scale = gains / col_norm
    moment_all = lax.all_gather(in_moment, "dp", axis=3, tiled=True)

    i_hi = input_factor.astype(BF)
    start = lax.axis_index("expert") * experts_here
    gate = lax.dynamic_slice_in_dim(g.reshape(n_all, lanes), start, experts_here, 1)
    gate = gate.T[:, :, None]

    projected = mm("td,jpdf->jptf", x, merged)
    gate_pre = projected[:, 0]
    up_pre = projected[:, 1]
    s = jax.nn.sigmoid(gate_pre)
    hidden = (gate_pre * s * up_pre * gate).astype(BF)
    grad_hidden = mm("td,jfd->jtf", c, w_down) * gate
    grad_gate = (grad_hidden * up_pre * s * (1.0 + gate_pre * (1.0 - s))).astype(BF)
    grad_up = (grad_hidden * gate_pre * s).astype(BF)
    grad_pair = jnp.stack([grad_gate, grad_up], axis=1)
    part_mixed = mm("jtf,jfd->td", hidden, w_down).astype(BF)
    part_grad = mm("jptf,jpdf->td", grad_pair, merged).astype(BF)
    split = (4 * nz, tok_here, width)
    mixed, token_grad = scatter(nz, part_mixed.reshape(split), part_grad.reshape(split))

    act_sum = jnp.sum(grad_pair.astype(F32) * projected, axis=2)
    gain_grad = act_sum / gains
    curvature = act_sum / norm2
    scaled_out = output_factor * col_scale[:, :, None, :]
    tilted = output_factor * (curvature / col_scale)[:, :, None, :]
    t_rows = mm("jptf,jprf->jptr", grad_pair, scaled_out.astype(BF))
    in_part = ADAPTER_SCALE * (
        mm("jptr,td->jprd", t_rows.astype(BF), x)
        - mm("jprf,jpdf->jprd", tilted.astype(BF), merged)
    )
    low_rows = mm("td,jprd->jptr", x, i_hi)
    out_grad = ADAPTER_SCALE * (
        mm("jptr,jptf->jprf", low_rows.astype(BF), grad_pair) * col_scale[:, :, None, :]
        - mm("jprd,jpdf->jprf", i_hi, merged) * (curvature / col_scale)[:, :, None, :]
    )
    n_dp = lax.axis_size("dp")
    mine = in_part
    pieces = lax.all_gather(mine, "dp", axis=0)
    in_grad = pieces[0]
    for k in range(1, n_dp):
        in_grad = in_grad + pieces[k]
    new_mom_all = MOMENTUM * moment_all + in_grad
    return (mixed, token_grad) + update(
        new_mom_all, out_grad, gain_grad, input_factor, output_factor, gains,
        in_moment, out_moment, gain_moment,
    )


def solution(mesh):
    return jax.shard_map(
        body,
        mesh=mesh,
        in_specs=(
            P(("groups", "expert", "dp"), None),
            P(("groups", "expert", "dp"), None),
            P(("groups", "expert", "dp"), None),
            P(("groups", "expert", "dp"), None),
            P(("groups", "expert", "dp"), None),
            P("expert", None, None, "dp"),
            P("expert", "dp", None),
            P("expert", None, None, None),
            P("expert", None, None, "dp"),
            P("expert", None, "dp"),
            P("expert", None, None, "dp"),
            P("expert", None, None, "dp"),
            P("expert", None, "dp"),
        ),
        out_specs=(
            P(("groups", "expert", "dp"), None),
            P(("groups", "expert", "dp"), None),
            P(("groups", "expert"), None, None, None),
            P(("groups", "expert"), None, None, "dp"),
            P(("groups", "expert"), None, None, "dp"),
            P(("groups", "expert"), None, None, "dp"),
            P(("groups", "expert"), None, "dp"),
            P(("groups", "expert"), None, "dp"),
        ),
        check_vma=False,
    )
```
